256 devices in a mesh: expert: 8 (over x, core), dp: 8 (over z), pipe: 4 (over y).
Axes of the slice: x: 4, y: 4, z: 8, core: 2. Of those that a mesh axis runs over, the one named last changes fastest.
Arguments:
- tokens: bfloat16 [2048, 3072], P(('expert', 'dp'), 'pipe'), may hold values from -6 to 6
- out_grad: bfloat16 [2048, 3072], P(('expert', 'dp'), 'pipe'), may hold values from -6 to 6
- gate_values: float32 [2048, 2], P(('expert', 'dp')), may hold values from 0.1 to 1
- expert_ids: int32 [2048, 2], P(('expert', 'dp')), may hold values from 0 to 7, all different within a row; in each aligned block of 32 rows (0 to 31, 32 to 63, ...) at most 16 rows name the same one
- w_gate: bfloat16 [8, 3072, 8192], P('expert', None, ('dp', 'pipe')), may hold values from -0.109375 to 0.109375
- w_up: bfloat16 [8, 3072, 8192], P('expert', None, ('dp', 'pipe')), may hold values from -0.109375 to 0.109375
- w_down: bfloat16 [8, 8192, 3072], P('expert', ('dp', 'pipe')), may hold values from -0.0625 to 0.0625
Outputs:
- grad_tokens: bfloat16 [2048, 3072], P(('expert', 'dp'), 'pipe')
- gate_weight_gradient: bfloat16 [8, 3072, 8192], P('expert', None, ('dp', 'pipe'))
- up_weight_gradient: bfloat16 [8, 3072, 8192], P('expert', None, ('dp', 'pipe'))
- grad_down: bfloat16 [8, 8192, 3072], P('expert', ('dp', 'pipe'))
The draws below stay inside these ranges and needn't reach their ends.
Inputs may be any that keep to these rules, and one draw needn't show every extreme that they name: `expert_ids`: each token names two different experts; among the 32 tokens of one block no expert is named more than 16 times, and in some blocks one is named exactly 16 times.
All inputs are finite; a program needn't handle non-finite values.
Results may differ from the reference program's by a relative error of at most 0.0065.
Values may be sent and summed in bfloat16 or wider, within the bound.
No kernel may reach another device: no remote copies, remote signals or barrier semaphores. Data moves between devices by JAX's collectives and lax.ppermute only.
A program may use at most 128 MiB of HBM per device.

```python
import math
import jax
import jax.numpy as jnp
import numpy as np
from jax import lax

D = 3072
FF = 8192
TOK_DEV = 32
EXPERTS = 8
CAP = 16
TOKENS = 2048
N_EXPERT = 8
N_DP = 8


def level_of(own_key, extent, pieces, smallest, largest):
    level = 1.0
    for axis_at, parts in pieces:
        steps = jax.random.uniform(jax.random.fold_in(jax.random.fold_in(own_key, 6), axis_at), (parts,), jnp.float32, smallest / len(pieces), largest / len(pieces))
        level = level * jnp.repeat(jnp.exp(steps), extent[axis_at] // parts).reshape((-1,) + (1,) * (len(extent) - 1 - axis_at))
    return level


def deal_out(stream_key, own, number, rows, count, top, bound, lean):
    order = jax.random.permutation(stream_key, count)
    packed, usual = shares(count, rows * top, bound, lean, True), shares(count, rows * top, bound, lean, False)
    places = jnp.arange(count)

    def named(tallies, rotation):
        used = int((tallies > 0).sum())
        fixed = max(1, used // 4)
        shifted = fixed + (places - fixed + rotation * (used - fixed)) % max(1, count - fixed)
        return jnp.zeros((count,), jnp.int32).at[order[jnp.where(places < fixed, places, shifted)]].set(jnp.asarray(tallies, jnp.int32))

    tallies = jnp.where(number % 4 == 0, named(packed, number // 4), named(usual, number - number // 4 - 1))
    mixed = jax.random.permutation(jax.random.fold_in(own, 3), count)
    donor, taker = mixed[0:count // 2 * 2:2], mixed[1:count // 2 * 2:2]
    slack = jnp.minimum(tallies[donor] - 1, bound - tallies[taker]) // 2
    slack = jnp.where((donor == order[0]) | (taker == order[0]) | (tallies[taker] == 0), 0, jnp.maximum(slack, 0))
    shifted = jax.random.randint(jax.random.fold_in(own, 4), (count // 2,), 0, 1 << 20) % (slack + 1)
    tallies = tallies.at[donor].add(-shifted).at[taker].add(shifted)
    items = jnp.searchsorted(jnp.cumsum(tallies), jnp.arange(rows * top), side="right").astype(jnp.int32)
    grid = items.reshape(top, rows).T
    grid = grid[jax.random.permutation(jax.random.fold_in(own, 1), rows)]
    rotation = jax.random.randint(jax.random.fold_in(own, 2), (rows, 1), 0, top)
    return jnp.take_along_axis(grid, (jnp.arange(top)[None, :] + rotation) % top, axis=1)


def shares(number_of, total, bound, lean, full):
    weights = [(1 << 20) // math.isqrt(grade ** lean) + 1 for grade in range(1, number_of + 1)]
    largest = bound if full else min(bound, max(-(-total // number_of), total * weights[0] // sum(weights)))
    least = 1 if total - largest >= number_of - 1 else 0
    holding, surplus = [largest] + [least] * (number_of - 1), total - largest - least * (number_of - 1)
    while surplus > 0:
        candidates = [i for i in range(1, number_of) if holding[i] < largest] or [i for i in range(1, number_of) if holding[i] < bound]
        pool, left = sum([weights[i] for i in candidates]), surplus
        for i in candidates:
            extra = min(bound - holding[i], max(1, left * weights[i] // pool), surplus)
            holding[i] = holding[i] + extra
            surplus = surplus - extra
    return np.array(holding)


def normal_values(own_key, shape, spread, limit, cuts=(), kind=jnp.bfloat16):
    level = level_of(own_key, shape, cuts, -0.22, 0.18) if cuts else 1.0
    values = jax.random.normal(own_key, shape, jnp.float32) * spread * level
    return jnp.minimum(jnp.maximum(values, -limit), limit).astype(kind)


def setup_inputs(seed: int = 0) -> dict:
    key_list = jax.random.split(jax.random.key(seed), 8)
    tokens = normal_values(key_list[0], (TOKENS, D), 1.0, 6.0, ((0, 64), (1, 4)))
    out_grad = normal_values(key_list[1], (TOKENS, D), 1.0, 6.0, ((0, 64), (1, 4)))
    gate_values = jnp.clip(0.1 + 0.9 * jax.random.uniform(key_list[2], (TOKENS, 2), jnp.float32) ** level_of(key_list[2], (TOKENS, 2), ((0, 64),), -0.2, 0.2), 0.1, 1.0)
    expert_ids_keys = jax.random.split(jax.random.fold_in(key_list[3], 1), TOKENS // TOK_DEV)
    expert_ids_turns = jax.random.permutation(jax.random.fold_in(key_list[3], 3), TOKENS // TOK_DEV)
    expert_ids = jax.vmap(lambda own, number: deal_out(jax.random.fold_in(key_list[3], 2), own, number, TOK_DEV, EXPERTS, 2, CAP, 2))(expert_ids_keys, expert_ids_turns).reshape((TOKENS, 2))
    w_gate = normal_values(key_list[4], (EXPERTS, D, FF), D ** -0.5, 0.109375, ((0, 8), (2, 32)))
    w_up = normal_values(key_list[5], (EXPERTS, D, FF), D ** -0.5, 0.109375, ((0, 8), (2, 32)))
    w_down = normal_values(key_list[6], (EXPERTS, FF, D), FF ** -0.5, 0.0625, ((0, 8), (1, 32)))
    return {"tokens": tokens, "out_grad": out_grad, "gate_values": gate_values, "expert_ids": expert_ids, "w_gate": w_gate, "w_up": w_up, "w_down": w_down}


def slot_positions(expert_ids):
    owners = N_EXPERT * N_DP
    choices_flat = expert_ids.reshape(owners, 2 * TOK_DEV)
    one_hot = (choices_flat[:, :, None] == jnp.arange(EXPERTS, dtype=jnp.int32)[None, None, :]).astype(jnp.int32)
    ranks = jnp.cumsum(one_hot, axis=1) - 1
    return choices_flat, jnp.sum(one_hot * ranks, axis=2).astype(jnp.int32)


def reference(tokens, out_grad, gate_values, expert_ids, w_gate, w_up, w_down):
    owners = N_EXPERT * N_DP
    choices_flat, positions = slot_positions(expert_ids)
    owner_index = jnp.arange(owners, dtype=jnp.int32)[:, None]
    target = ((choices_flat * owners + owner_index) * CAP + positions).astype(jnp.int32)
    source = (owner_index * (2 * TOK_DEV) + jnp.arange(2 * TOK_DEV, dtype=jnp.int32)[None, :]).astype(jnp.int32)
    table = jnp.full((EXPERTS * owners * CAP,), -1, jnp.int32)
    table = table.at[target.reshape(-1)].set(source.reshape(-1)).reshape(EXPERTS, owners * CAP)
    scaled = (gate_values[:, :, None] * out_grad.astype(jnp.float32)[:, None, :]).astype(jnp.bfloat16)
    scaled = scaled.reshape(2 * TOKENS, D)

    def one_expert(operands):
        slot_rows, gate_mat, up_mat, down_mat = operands
        live = slot_rows >= 0
        safe_rows = jnp.where(live, slot_rows, 0).astype(jnp.int32)
        feats = jnp.where(live[:, None], tokens[safe_rows // 2], 0)
        cotangent = jnp.where(live[:, None], scaled[safe_rows], 0)
        gate_pre = jnp.dot(feats, gate_mat, preferred_element_type=jnp.float32)
        up_preactivation = jnp.dot(feats, up_mat, preferred_element_type=jnp.float32)
        act_grad = jnp.dot(cotangent, down_mat.T, preferred_element_type=jnp.float32)
        sigmoid_gate = jax.nn.sigmoid(gate_pre)
        linear = gate_pre * sigmoid_gate
        swiglu_activation = (linear * up_preactivation).astype(jnp.bfloat16)
        slope_term = sigmoid_gate * (1.0 + gate_pre * (1.0 - sigmoid_gate))
        gate_output_gradient = (act_grad * up_preactivation * slope_term).astype(jnp.bfloat16)
        up_output_gradient = (act_grad * linear).astype(jnp.bfloat16)
        gate_weight_gradient = jnp.dot(feats.T, gate_output_gradient, preferred_element_type=jnp.float32).astype(jnp.bfloat16)
        up_weight_gradient = jnp.dot(feats.T, up_output_gradient, preferred_element_type=jnp.float32).astype(jnp.bfloat16)
        grad_down = jnp.dot(swiglu_activation.T, cotangent, preferred_element_type=jnp.float32).astype(jnp.bfloat16)
        slot_grad = (jnp.dot(gate_output_gradient, gate_mat.T, preferred_element_type=jnp.float32)
                     + jnp.dot(up_output_gradient, up_mat.T, preferred_element_type=jnp.float32)).astype(jnp.bfloat16)
        return gate_weight_gradient, up_weight_gradient, grad_down, slot_grad

    gate_weight_gradient, up_weight_gradient, grad_down, slot_grad = lax.map(one_expert, (table, w_gate, w_up, w_down))
    live_all = (table >= 0).reshape(-1)
    token_index = jnp.where(live_all, table.reshape(-1) // 2, 0).astype(jnp.int32)
    contrib = jnp.where(live_all[:, None], slot_grad.reshape(-1, D).astype(jnp.float32), 0.0)
    grad_tokens = jnp.zeros((TOKENS, D), jnp.float32).at[token_index].add(contrib).astype(jnp.bfloat16)
    return grad_tokens, gate_weight_gradient, up_weight_gradient, grad_down
```

```python
import functools

import jax
import jax.numpy as jnp
from jax import lax
from jax.experimental import pallas as pl
from jax.experimental.pallas import tpu as pltpu
from jax.sharding import PartitionSpec as P

F32 = jnp.float32
BF16 = jnp.bfloat16
INTERPRET = False
VMEM_LIMIT = 58 * 1024 * 1024
NN = (((1,), (0,)), ((), ()))
NT = (((1,), (1,)), ((), ()))


def dot(a, b, dims=NN):
    return lax.dot_general(a, b, dims, preferred_element_type=F32)


def slot_indices(expert_ids, expert_count, capacity):
    choices_flat = expert_ids.reshape(-1)
    one_hot = (choices_flat[:, None] == jnp.arange(expert_count, dtype=jnp.int32)[None, :]).astype(
        jnp.int32
    )
    ranks = jnp.cumsum(one_hot, axis=0) - 1
    return (choices_flat * capacity + jnp.sum(one_hot * ranks, axis=1)).reshape(-1, 2)


def fill_slots(slot_index, gate_values, slot_total, features, cotangent):
    hits = jnp.arange(slot_total, dtype=jnp.int32)[:, None, None] == slot_index[None, :, :]
    picker = jnp.any(hits, axis=2).astype(BF16)
    weighting = jnp.sum(jnp.where(hits, gate_values[None, :, :], 0.0), axis=2)
    sent_rows = jnp.dot(picker, features, preferred_element_type=F32).astype(BF16)
    sent_grads = jnp.dot(weighting, cotangent.astype(F32), precision=lax.Precision.HIGHEST).astype(
        BF16
    )
    return (picker, sent_rows, sent_grads)


def expert_kernel(expert_count, x_ref, wg_ref, wu_ref, wd_ref, act_ref, gg_ref, ug_ref, ring_ref, cross_ref):
    groups, pipes, both, feat = x_ref.shape
    rows = both // 2
    total = groups * rows
    half = feat // 2
    capacity = rows // expert_count
    gate = up = act_grad = None
    for p in range(pipes):
        features = x_ref[:, p, :rows, :].reshape(total, feat)
        cotangent = x_ref[:, p, rows:, :].reshape(total, feat)
        cols = slice(p * feat, (p + 1) * feat)
        g = dot(features, wg_ref[cols, :])
        u = dot(features, wu_ref[cols, :])
        a = dot(cotangent, wd_ref[:, cols], NT)
        gate = g if gate is None else gate + g
        up = u if up is None else up + u
        act_grad = a if act_grad is None else act_grad + a
    sig = jax.nn.sigmoid(gate)
    linear = gate * sig
    act = (linear * up).astype(BF16)
    gate_grad = (act_grad * up * (sig * (1.0 + gate * (1.0 - sig)))).astype(BF16)
    up_grad = (act_grad * linear).astype(BF16)
    act_ref[...] = act.T
    gg_ref[...] = gate_grad.T
    ug_ref[...] = up_grad.T
    for p in range(pipes):
        cols = slice(p * feat, (p + 1) * feat)
        back = (dot(gate_grad, wg_ref[cols, :], NT) + dot(up_grad, wu_ref[cols, :], NT)).astype(BF16)
        ring_ref[p] = back[:, :half]
        for d in range(groups):
            part = back[d * rows : (d + 1) * rows, half:]
            cross_ref[:, p, d * capacity : (d + 1) * capacity, :] = part.reshape(
                expert_count, capacity, half
            )


def run_expert(x, wg, wu, wd, expert_count, step_groups):
    groups, pipes, both, feat = x.shape
    rows = both // 2
    width, hidden = wg.shape
    half = feat // 2
    step_rows = step_groups * rows
    step_slots = step_rows // expert_count
    everything = groups * rows
    whole = lambda shape: pl.BlockSpec(shape, lambda s: (0, 0))
    flipped = pl.BlockSpec((hidden, step_rows), lambda s: (0, s))
    return pl.pallas_call(
        functools.partial(expert_kernel, expert_count),
        grid=(groups // step_groups,),
        in_specs=[
            pl.BlockSpec((step_groups, pipes, both, feat), lambda s: (s, 0, 0, 0)),
            whole((width, hidden)),
            whole((width, hidden)),
            whole((hidden, width)),
        ],
        out_specs=[
            flipped,
            flipped,
            flipped,
            pl.BlockSpec((pipes, step_rows, half), lambda s: (0, s, 0)),
            pl.BlockSpec((expert_count, pipes, step_slots, half), lambda s: (0, 0, s, 0)),
        ],
        out_shape=[jax.ShapeDtypeStruct((hidden, everything), BF16)] * 3
        + [
            jax.ShapeDtypeStruct((pipes, everything, half), BF16),
            jax.ShapeDtypeStruct((expert_count, pipes, everything // expert_count, half), BF16),
        ],
        compiler_params=pltpu.CompilerParams(vmem_limit_bytes=VMEM_LIMIT),
        name="expert",
        interpret=INTERPRET,
    )(x, wg, wu, wd)


def weight_kernel(x_ref, act_ref, gg_ref, ug_ref, dwg_ref, dwu_ref, dwd_ref):
    groups, _, both, feat = x_ref.shape
    rows = both // 2
    features = x_ref[:, 0, :rows, :].reshape(groups * rows, feat)
    cotangent = x_ref[:, 0, rows:, :].reshape(groups * rows, feat)
    dwg_ref[...] = dot(gg_ref[...], features).astype(BF16).T
    dwu_ref[...] = dot(ug_ref[...], features).astype(BF16).T
    dwd_ref[...] = dot(act_ref[...], cotangent).astype(BF16)


def run_weights(x, act, gg, ug):
    groups, pipes, both, feat = x.shape
    hidden, everything = act.shape
    whole = pl.BlockSpec((hidden, everything), lambda p: (0, 0))
    return pl.pallas_call(
        weight_kernel,
        grid=(pipes,),
        in_specs=[
            pl.BlockSpec((groups, 1, both, feat), lambda p: (0, p, 0, 0)),
            whole,
            whole,
            whole,
        ],
        out_specs=[
            pl.BlockSpec((feat, hidden), lambda p: (p, 0)),
            pl.BlockSpec((feat, hidden), lambda p: (p, 0)),
            pl.BlockSpec((hidden, feat), lambda p: (0, p)),
        ],
        out_shape=[
            jax.ShapeDtypeStruct((pipes * feat, hidden), BF16),
            jax.ShapeDtypeStruct((pipes * feat, hidden), BF16),
            jax.ShapeDtypeStruct((hidden, pipes * feat), BF16),
        ],
        compiler_params=pltpu.CompilerParams(vmem_limit_bytes=VMEM_LIMIT),
        name="weights",
        interpret=INTERPRET,
    )(x, act, gg, ug)


def combine_kernel(group_count, x_ref, slots_ref, out_ref):
    experts, _, slots, half = x_ref.shape
    capacity = slots // group_count
    tokens = slots_ref.shape[1]
    want = lax.broadcasted_iota(jnp.int32, (tokens, experts * capacity), 1)
    for d in range(group_count):
        rows = x_ref[:, 0, d * capacity : (d + 1) * capacity, :].reshape(experts * capacity, half)
        picked = (slots_ref[d, :, 0:1] == want) | (slots_ref[d, :, 1:2] == want)
        chosen = jnp.where(picked, 1.0, 0.0).astype(BF16)
        out_ref[0, d * tokens : (d + 1) * tokens, :] = dot(chosen, rows).astype(BF16)


def total_of(parts):
    total = parts[0].astype(F32)
    for k in range(1, parts.shape[0]):
        total = total + parts[k].astype(F32)
    return total.astype(BF16)


def run_combine(x, slots):
    experts, pipes, everything, half = x.shape
    group_count, tokens, _ = slots.shape
    return pl.pallas_call(
        functools.partial(combine_kernel, group_count),
        grid=(pipes,),
        in_specs=[
            pl.BlockSpec((experts, 1, everything, half), lambda p: (0, p, 0, 0)),
            pl.BlockSpec((group_count, tokens, 2), lambda p: (0, 0, 0)),
        ],
        out_specs=pl.BlockSpec((1, group_count * tokens, half), lambda p: (p, 0, 0)),
        out_shape=jax.ShapeDtypeStruct((pipes, group_count * tokens, half), BF16),
        compiler_params=pltpu.CompilerParams(vmem_limit_bytes=VMEM_LIMIT),
        name="combine",
        interpret=INTERPRET,
    )(x, slots)


def body(tokens, out_grad, gate_values, expert_ids, w_gate, w_up, w_down):
    expert_count = lax.axis_size("expert")
    group_count = lax.axis_size("dp")
    pipe_count = lax.axis_size("pipe")
    token_count, feat = tokens.shape
    capacity = max(token_count // 2, 2 * token_count // expert_count)
    slot_total = expert_count * capacity
    half = feat // 2
    slot_index = slot_indices(expert_ids, expert_count, capacity)
    picker, sent_rows, sent_grads = fill_slots(
        slot_index, gate_values, slot_total, tokens, out_grad
    )
    sent = jnp.concatenate(
        [
            sent_rows.reshape(expert_count, 1, capacity, feat),
            sent_grads.reshape(expert_count, 1, capacity, feat),
        ],
        axis=1,
    )
    received = lax.all_to_all(sent, "expert", split_axis=0, concat_axis=0, tiled=True)
    received = received.transpose(1, 0, 2, 3).reshape(1, 2 * slot_total, feat)
    gathered = lax.all_gather(received, ("dp", "pipe"), axis=0, tiled=True)
    column_slots = lax.all_gather(slot_index[None], "dp", axis=0, tiled=True)
    gathered, column_slots = lax.optimization_barrier((gathered, column_slots))
    x = gathered.reshape(group_count, pipe_count, 2 * slot_total, feat)
    act, gg, ug, ring, cross = run_expert(
        x, w_gate[0], w_up[0], w_down[0], expert_count, group_count // 4
    )
    over_pipe = lax.psum_scatter(ring, "pipe", scatter_dimension=0, tiled=True)
    crossed = lax.all_to_all(cross, "expert", split_axis=0, concat_axis=0, tiled=True)
    gate_weight_gradient, up_weight_gradient, grad_down = run_weights(x, act, gg, ug)
    summed = lax.psum_scatter(
        over_pipe.reshape(group_count, slot_total, half), "dp", scatter_dimension=0, tiled=True
    )
    column = run_combine(crossed, column_slots)
    column = lax.all_to_all(column, "pipe", split_axis=0, concat_axis=0, tiled=True)
    column = total_of(column)
    column = lax.all_to_all(
        column.reshape(group_count, token_count, half), "dp", split_axis=0, concat_axis=0, tiled=True
    )
    right = total_of(column)
    returned = lax.all_to_all(
        summed.reshape(expert_count, capacity, half), "expert", split_axis=0, concat_axis=0, tiled=True
    )
    left = jnp.einsum(
        "st,sq->tq", picker, returned.reshape(slot_total, half), preferred_element_type=F32
    ).astype(BF16)
    grad_tokens = jnp.concatenate([left, right], axis=1)
    return (
        grad_tokens,
        gate_weight_gradient[None],
        up_weight_gradient[None],
        grad_down[None],
    )


def solution(mesh):
    rows = P(("expert", "dp"), "pipe")
    pairs = P(("expert", "dp"), None)
    wide = P("expert", None, ("dp", "pipe"))
    tall = P("expert", ("dp", "pipe"), None)
    return jax.shard_map(
        body,
        mesh=mesh,
        in_specs=(rows, rows, pairs, pairs, wide, wide, tall),
        out_specs=(rows, wide, wide, tall),
        check_vma=False,
    )
```

```python
import functools

import jax
import jax.numpy as jnp
from jax import lax
from jax.experimental import pallas as pl
from jax.experimental.pallas import tpu as pltpu
from jax.sharding import PartitionSpec as P


F32 = jnp.float32
BF16 = jnp.bfloat16
INTERPRET = False
VMEM_LIMIT = 58 * 1024 * 1024
NN = (((1,), (0,)), ((), ()))
NT = (((1,), (1,)), ((), ()))


def dot(a, b, dims=NN):
    return lax.dot_general(a, b, dims, preferred_element_type=F32)


def slot_indices(expert_ids, expert_count, capacity):
    choices_flat = expert_ids.reshape(-1)
    one_hot = (choices_flat[:, None] == jnp.arange(expert_count, dtype=jnp.int32)[None, :]).astype(
        jnp.int32
    )
    ranks = jnp.cumsum(one_hot, axis=0) - 1
    return (choices_flat * capacity + jnp.sum(one_hot * ranks, axis=1)).reshape(-1, 2)


def fill_slots(slot_index, gate_values, slot_total, features, cotangent):
    hits = jnp.arange(slot_total, dtype=jnp.int32)[:, None, None] == slot_index[None, :, :]
    picker = jnp.any(hits, axis=2).astype(BF16)
    weighting = jnp.sum(jnp.where(hits, gate_values[None, :, :], 0.0), axis=2)
    sent_rows = jnp.dot(picker, features, preferred_element_type=F32).astype(BF16)
    sent_grads = jnp.dot(weighting, cotangent.astype(F32), precision=lax.Precision.HIGHEST).astype(
        BF16
    )
    return (picker, sent_rows, sent_grads)


def expert_kernel(expert_count, order_ref, a_ref, b0_ref, b1_ref, b3_ref, b2x_ref, b2y_ref, wg_ref, wu_ref, wd_ref, act_ref, gg_ref, ug_ref, ring_ref, cross_ref):
    groups, pipes, both, half = a_ref.shape
    rows = both // 2
    total = groups * rows
    feat = 2 * half
    capacity = rows // expert_count
    early = pl.program_id(0) < pl.num_programs(0) // 2
    pieces = []
    for p in range(pipes):
        pieces.append((a_ref[:, p], p * feat))
    opposite = jnp.where(early, b2x_ref[...], b2y_ref[...])
    for k, value in enumerate((b0_ref[...], b3_ref[...], opposite, b1_ref[...])):
        pieces.append((value, pl.multiple_of(order_ref[k] * feat + half, 128)))
    gate = up = act_grad = None
    for value, start in pieces:
        features = value[:, :rows, :].reshape(total, half)
        cotangent = value[:, rows:, :].reshape(total, half)
        cols = pl.ds(start, half)
        g = dot(features, wg_ref[cols, :])
        u = dot(features, wu_ref[cols, :])
        a = dot(cotangent, wd_ref[:, cols], NT)
        gate = g if gate is None else gate + g
        up = u if up is None else up + u
        act_grad = a if act_grad is None else act_grad + a
    sig = jax.nn.sigmoid(gate)
    linear = gate * sig
    act = (linear * up).astype(BF16)
    gate_grad = (act_grad * up * (sig * (1.0 + gate * (1.0 - sig)))).astype(BF16)
    up_grad = (act_grad * linear).astype(BF16)
    act_ref[...] = act.T
    gg_ref[...] = gate_grad.T
    ug_ref[...] = up_grad.T
    for p in range(pipes):
        cols = slice(p * feat, (p + 1) * feat)
        back = (dot(gate_grad, wg_ref[cols, :], NT) + dot(up_grad, wu_ref[cols, :], NT)).astype(BF16)
        for d in range(groups):
            part = back[d * rows : (d + 1) * rows].reshape(expert_count, capacity, feat)
            ring_ref[p, :, d * capacity : (d + 1) * capacity, :] = part[:, :, :half]
            cross_ref[:, p, d * capacity : (d + 1) * capacity, :] = part[:, :, half:]


def run_expert(order, a, b, wg, wu, wd, expert_count, step_groups):
    groups, pipes, both, half = a.shape
    rows = both // 2
    width, hidden = wg.shape
    step_rows = step_groups * rows
    step_slots = step_rows // expert_count
    everything = groups * rows
    steps = groups // step_groups
    whole = lambda shape: pl.BlockSpec(shape, lambda s, o: (0, 0))
    flipped = pl.BlockSpec((hidden, step_rows), lambda s, o: (0, s))
    piece = pl.BlockSpec((step_groups, both, half), lambda s, o: (s, 0, 0))
    return pl.pallas_call(
        functools.partial(expert_kernel, expert_count),
        grid_spec=pltpu.PrefetchScalarGridSpec(
            num_scalar_prefetch=1,
            grid=(steps,),
            in_specs=[
                pl.BlockSpec((step_groups, pipes, both, half), lambda s, o: (s, 0, 0, 0)),
                piece,
                piece,
                piece,
                pl.BlockSpec(
                    (step_groups, both, half), lambda s, o: (jnp.minimum(s, steps // 2 - 1), 0, 0)
                ),
                pl.BlockSpec(
                    (step_groups, both, half), lambda s, o: (jnp.maximum(s - steps // 2, 0), 0, 0)
                ),
                whole((width, hidden)),
                whole((width, hidden)),
                whole((hidden, width)),
            ],
            out_specs=[
                flipped,
                flipped,
                flipped,
                pl.BlockSpec((pipes, expert_count, step_slots, half), lambda s, o: (0, 0, s, 0)),
                pl.BlockSpec((expert_count, pipes, step_slots, half), lambda s, o: (0, 0, s, 0)),
            ],
        ),
        out_shape=[jax.ShapeDtypeStruct((hidden, everything), BF16)] * 3
        + [
            jax.ShapeDtypeStruct((pipes, expert_count, everything // expert_count, half), BF16),
            jax.ShapeDtypeStruct((expert_count, pipes, everything // expert_count, half), BF16),
        ],
        compiler_params=pltpu.CompilerParams(vmem_limit_bytes=VMEM_LIMIT),
        name="expert",
        interpret=INTERPRET,
    )(order, a, *b, wg, wu, wd)


def weight_kernel(order_ref, a_ref, b0_ref, b1_ref, b3_ref, b2x_ref, b2y_ref, act_ref, gg_ref, ug_ref, dwg_ref, dwu_ref, dwd_ref):
    groups, _, both, half = a_ref.shape
    rows = both // 2
    step = pl.program_id(0)
    count = pl.num_programs(0) // 2

    def work(value):
        features = value[:, :rows, :].reshape(groups * rows, half)
        cotangent = value[:, rows:, :].reshape(groups * rows, half)
        dwg_ref[...] = dot(gg_ref[...], features).astype(BF16).T
        dwu_ref[...] = dot(ug_ref[...], features).astype(BF16).T
        dwd_ref[...] = dot(act_ref[...], cotangent).astype(BF16)

    pl.when(step < count)(lambda: work(a_ref[:, 0]))
    pl.when(step == count)(lambda: work(b0_ref[...]))
    pl.when(step == count + 1)(lambda: work(b3_ref[...]))
    pl.when(step == count + 2)(
        lambda: work(jnp.concatenate([b2x_ref[...], b2y_ref[...]], axis=0))
    )
    pl.when(step == count + 3)(lambda: work(b1_ref[...]))


def run_weights(order, a, b, act, gg, ug):
    groups, pipes, both, half = a.shape
    hidden, everything = act.shape
    whole = pl.BlockSpec((hidden, everything), lambda s, o: (0, 0))
    piece = lambda v: pl.BlockSpec(v.shape, lambda s, o: (0, 0, 0))

    def place(s, o):
        return jnp.where(s < pipes, 2 * s, 2 * o[jnp.maximum(s - pipes, 0)] + 1)

    return pl.pallas_call(
        weight_kernel,
        grid_spec=pltpu.PrefetchScalarGridSpec(
            num_scalar_prefetch=1,
            grid=(2 * pipes,),
            in_specs=[
                pl.BlockSpec(
                    (groups, 1, both, half), lambda s, o: (0, jnp.minimum(s, pipes - 1), 0, 0)
                ),
            ]
            + [piece(v) for v in b]
            + [whole] * 3,
            out_specs=[
                pl.BlockSpec((half, hidden), lambda s, o: (place(s, o), 0)),
                pl.BlockSpec((half, hidden), lambda s, o: (place(s, o), 0)),
                pl.BlockSpec((hidden, half), lambda s, o: (0, place(s, o))),
            ],
        ),
        out_shape=[
            jax.ShapeDtypeStruct((2 * pipes * half, hidden), BF16),
            jax.ShapeDtypeStruct((2 * pipes * half, hidden), BF16),
            jax.ShapeDtypeStruct((hidden, 2 * pipes * half), BF16),
        ],
        compiler_params=pltpu.CompilerParams(vmem_limit_bytes=VMEM_LIMIT),
        name="weights",
        interpret=INTERPRET,
    )(order, a, *b, act, gg, ug)


def combine_kernel(x_ref, slots_ref, out_ref):
    experts, _, slots, half = x_ref.shape
    group_count = slots_ref.shape[0]
    capacity = slots // group_count
    tokens = out_ref.shape[1] // group_count
    want = lax.broadcasted_iota(jnp.int32, (experts * capacity, tokens), 0).astype(F32)
    for d in range(group_count):
        rows = x_ref[:, 0, d * capacity : (d + 1) * capacity, :].reshape(experts * capacity, half)
        ids = slots_ref[d].astype(F32)
        picked = (ids[0:1, :tokens] == want) | (ids[1:2, :tokens] == want)
        chosen = jnp.where(picked, 1.0, 0.0).astype(BF16)
        out_ref[0, d * tokens : (d + 1) * tokens, :] = dot(
            chosen, rows, (((0,), (0,)), ((), ()))
        ).astype(BF16)


def run_combine(x, slots, tokens):
    experts, pipes, everything, half = x.shape
    group_count = slots.shape[0]
    return pl.pallas_call(
        combine_kernel,
        grid=(pipes,),
        in_specs=[
            pl.BlockSpec((experts, 1, everything, half), lambda p: (0, p, 0, 0)),
            pl.BlockSpec(slots.shape, lambda p: (0, 0, 0)),
        ],
        out_specs=pl.BlockSpec((1, group_count * tokens, half), lambda p: (p, 0, 0)),
        out_shape=jax.ShapeDtypeStruct((pipes, group_count * tokens, half), BF16),
        compiler_params=pltpu.CompilerParams(vmem_limit_bytes=VMEM_LIMIT),
        name="combine",
        interpret=INTERPRET,
    )(x, slots)


def total_of(parts):
    total = parts[0].astype(F32)
    for k in range(1, parts.shape[0]):
        total = total + parts[k].astype(F32)
    return total.astype(BF16)


def shift(x, axis, by):
    count = lax.axis_size(axis)
    return lax.ppermute(x, axis, [(k, (k + by) % count) for k in range(count)])


def place_kernel(moves, at_ref, *refs):
    count = 1 + max(m[0] for m in moves)
    sems = refs[-1]
    copies = []
    for n, (source, begin, size, columns, target, place, row) in enumerate(moves):
        copies.append(
            pltpu.make_async_copy(
                refs[source].at[begin : begin + size, :columns],
                refs[count + target].at[at_ref[place], row : row + size, :],
                sems.at[n],
            )
        )
    for copy in copies:
        copy.start()
    for copy in copies:
        copy.wait()


def run_place(at, pieces, moves, shapes):
    return pl.pallas_call(
        functools.partial(place_kernel, moves),
        in_specs=[pl.BlockSpec(memory_space=pltpu.SMEM)]
        + [pl.BlockSpec(memory_space=pl.ANY)] * len(pieces),
        out_specs=[pl.BlockSpec(memory_space=pl.ANY)] * len(shapes),
        out_shape=[jax.ShapeDtypeStruct(shape, BF16) for shape in shapes],
        scratch_shapes=[pltpu.SemaphoreType.DMA((len(moves),))],
        compiler_params=pltpu.CompilerParams(vmem_limit_bytes=VMEM_LIMIT),
        name="place",
        interpret=INTERPRET,
    )(at, *pieces)


def groups_ring(x, rows):
    whole, width = x.shape
    cut = (whole // 2 + 15) // 16 * 16
    up1, down1 = shift(x, "dp", 1), shift(x, "dp", -1)
    up2, down2 = shift(up1, "dp", 1), shift(down1, "dp", -1)
    up3, down3 = shift(up2, "dp", 1), shift(down2, "dp", -1)
    far_up, far_down = shift(up3[:cut], "dp", 1), shift(down3[cut:], "dp", -1)
    count = lax.axis_size("dp")
    at = (lax.axis_index("dp") + jnp.arange(count, dtype=jnp.int32)) % count
    pieces = (x, down1, down2, down3, up3, up2, up1, far_up, far_down)
    moves = []
    for n, place in enumerate((0, 1, 2, 3, 5, 6, 7)):
        moves.append((n, 0, rows, width, 0, place, 0))
        moves.append((n, rows, whole - rows, 128, 1, place, 0))
    moves.append((7, 0, cut, width, 0, 4, 0))
    moves.append((8, 0, rows - cut, width, 0, 4, cut))
    moves.append((8, rows - cut, whole - rows, 128, 1, 4, 0))
    return run_place(at, pieces, tuple(moves), [(count, rows, width), (count, whole - rows, 128)])


def pipes_direct(x):
    pieces = (x, shift(x, "pipe", -1), shift(x, "pipe", 2), shift(x, "pipe", 1))
    count = lax.axis_size("pipe")
    at = (lax.axis_index("pipe") + jnp.arange(count, dtype=jnp.int32)) % count
    rows, width = x.shape
    moves = tuple((n, 0, rows, width, 0, n, 0) for n in range(count))
    return run_place(at, pieces, moves, [(count, rows, width)])[0]


def pipes_ring(x):
    cut = x.shape[0] // 2
    up1, down1 = shift(x, "pipe", 1), shift(x, "pipe", -1)
    return x, up1, down1, shift(up1[:cut], "pipe", 1), shift(down1[cut:], "pipe", -1)


def body(tokens, out_grad, gate_values, expert_ids, w_gate, w_up, w_down):
    expert_count = lax.axis_size("expert")
    group_count = lax.axis_size("dp")
    pipe_count = lax.axis_size("pipe")
    token_count, feat = tokens.shape
    capacity = max(token_count // 2, 2 * token_count // expert_count)
    slot_total = expert_count * capacity
    half = feat // 2
    slot_index = slot_indices(expert_ids, expert_count, capacity)
    _, sent_rows, sent_grads = fill_slots(slot_index, gate_values, slot_total, tokens, out_grad)
    sent = jnp.concatenate(
        [
            sent_rows.reshape(expert_count, 1, capacity, feat),
            sent_grads.reshape(expert_count, 1, capacity, feat),
        ],
        axis=1,
    )
    received = lax.all_to_all(sent, "expert", split_axis=0, concat_axis=0, tiled=True)
    received = received.transpose(1, 0, 2, 3).reshape(2 * slot_total, feat)
    slots = jnp.pad(slot_index.T.astype(BF16), ((0, 14), (0, half - token_count)))
    ringed, column_slots = groups_ring(
        jnp.concatenate([received[:, half:], slots], axis=0), 2 * slot_total
    )
    b = pipes_ring(ringed)
    a = lax.all_gather(pipes_direct(received[:, :half])[None], "dp", axis=0, tiled=True)
    me = lax.axis_index("pipe")
    order = (me + jnp.arange(pipe_count, dtype=jnp.int32)) % pipe_count
    act, gg, ug, ring, cross = run_expert(
        order, a, b, w_gate[0], w_up[0], w_down[0], expert_count, group_count // 4
    )
    over_pipe = lax.psum_scatter(
        ring.reshape(pipe_count, -1, half), "pipe", scatter_dimension=0, tiled=True
    )
    crossed = lax.all_to_all(cross, "expert", split_axis=0, concat_axis=0, tiled=True)
    gate_weight_gradient, up_weight_gradient, grad_down = run_weights(order, a, b, act, gg, ug)
    crossed, gate_weight_gradient = lax.optimization_barrier((crossed, gate_weight_gradient))
    right = run_combine(crossed, column_slots, token_count)
    right = lax.all_to_all(right, "pipe", split_axis=0, concat_axis=0, tiled=True)
    right = total_of(right)
    left = lax.all_to_all(
        over_pipe.reshape(expert_count, 1, -1, half), "expert", split_axis=0, concat_axis=0, tiled=True
    )
    left = run_combine(left, column_slots, token_count)[0]
    column = jnp.concatenate([left, right], axis=1).reshape(group_count, token_count, feat)
    column = lax.all_to_all(column, "dp", split_axis=0, concat_axis=0, tiled=True)
    return (
        total_of(column),
        gate_weight_gradient[None],
        up_weight_gradient[None],
        grad_down[None],
    )


def solution(mesh):
    rows = P(("expert", "dp"), "pipe")
    pairs = P(("expert", "dp"), None)
    wide = P("expert", None, ("dp", "pipe"))
    tall = P("expert", ("dp", "pipe"), None)

    return jax.shard_map(
        body,
        mesh=mesh,
        in_specs=(rows, rows, pairs, pairs, wide, wide, tall),
        out_specs=(rows, wide, wide, tall),
        check_vma=False,
    )
```

```python
import functools

import jax
import jax.numpy as jnp
from jax import lax
from jax.experimental import pallas as pl
from jax.experimental.pallas import tpu as pltpu
from jax.sharding import PartitionSpec as P

F32 = jnp.float32
BF16 = jnp.bfloat16
INTERPRET = False
MIB = 1024 * 1024
NN = (((1,), (0,)), ((), ()))
NT = (((1,), (1,)), ((), ()))


def dot(a, b, dims=NN):
    return lax.dot_general(a, b, dims, preferred_element_type=F32)


def slot_indices(expert_ids, expert_count, capacity):
    choices_flat = expert_ids.reshape(-1)
    one_hot = (choices_flat[:, None] == jnp.arange(expert_count, dtype=jnp.int32)[None, :]).astype(
        jnp.int32
    )
    ranks = jnp.cumsum(one_hot, axis=0) - 1
    return (choices_flat * capacity + jnp.sum(one_hot * ranks, axis=1)).reshape(-1, 2)


def fill_slots(slot_index, gate_values, slot_total, features, cotangent):
    hits = jnp.arange(slot_total, dtype=jnp.int32)[:, None, None] == slot_index[None, :, :]
    picker = jnp.any(hits, axis=2).astype(BF16)
    weighting = jnp.sum(jnp.where(hits, gate_values[None, :, :], 0.0), axis=2)
    sent_rows = jnp.dot(picker, features, preferred_element_type=F32).astype(BF16)
    sent_grads = jnp.dot(weighting, cotangent.astype(F32), precision=lax.Precision.HIGHEST).astype(
        BF16
    )
    return (picker, sent_rows, sent_grads)


def project_kernel(x_ref, wg_ref, wu_ref, gate_ref, up_ref):
    groups, pipes, rows, feat = x_ref.shape
    total = groups * rows
    gate = up = None
    for p in range(pipes):
        features = x_ref[:, p].reshape(total, feat)
        cols = slice(p * feat, (p + 1) * feat)
        g = dot(features, wg_ref[cols, :])
        u = dot(features, wu_ref[cols, :])
        gate = g if gate is None else gate + g
        up = u if up is None else up + u
    gate_ref[...] = gate
    up_ref[...] = up


def run_project(x, wg, wu, step_groups):
    groups, pipes, rows, feat = x.shape
    width, hidden = wg.shape
    step_rows = step_groups * rows
    whole = pl.BlockSpec((width, hidden), lambda s: (0, 0))
    result = pl.BlockSpec((step_rows, hidden), lambda s: (s, 0))
    return pl.pallas_call(
        project_kernel,
        grid=(groups // step_groups,),
        in_specs=[
            pl.BlockSpec((step_groups, pipes, rows, feat), lambda s: (s, 0, 0, 0)),
            whole,
            whole,
        ],
        out_specs=[result, result],
        out_shape=[jax.ShapeDtypeStruct((groups * rows, hidden), F32)] * 2,
        compiler_params=pltpu.CompilerParams(vmem_limit_bytes=58 * MIB),
        name="project",
        interpret=INTERPRET,
    )(x, wg, wu)


def expert_kernel(expert_count, order_ref, gate_ref, up_ref, c0_ref, c1_ref, c3_ref, c2x_ref, c2y_ref, wg_ref, wu_ref, wd_ref, act_ref, gg_ref, ug_ref, ring_ref, cross_ref):
    groups, rows, feat = c0_ref.shape
    pipes = wg_ref.shape[0] // feat
    total = groups * rows
    half = feat // 2
    capacity = rows // expert_count
    early = pl.program_id(0) < pl.num_programs(0) // 2
    opposite = jnp.where(early, c2x_ref[...], c2y_ref[...])
    act_grad = None
    for k, value in enumerate((c0_ref[...], c3_ref[...], opposite, c1_ref[...])):
        cols = pl.ds(pl.multiple_of(order_ref[k] * feat, 128), feat)
        a = dot(value.reshape(total, feat), wd_ref[:, cols], NT)
        act_grad = a if act_grad is None else act_grad + a
    gate = gate_ref[...]
    up = up_ref[...]
    sig = jax.nn.sigmoid(gate)
    linear = gate * sig
    act = (linear * up).astype(BF16)
    gate_grad = (act_grad * up * (sig * (1.0 + gate * (1.0 - sig)))).astype(BF16)
    up_grad = (act_grad * linear).astype(BF16)
    act_ref[...] = act.T
    gg_ref[...] = gate_grad.T
    ug_ref[...] = up_grad.T
    for p in range(pipes):
        cols = slice(p * feat, (p + 1) * feat)
        back = (dot(gate_grad, wg_ref[cols, :], NT) + dot(up_grad, wu_ref[cols, :], NT)).astype(BF16)
        ring_ref[p] = back[:, :half]
        for d in range(groups):
            part = back[d * rows : (d + 1) * rows, half:]
            cross_ref[:, p, d * capacity : (d + 1) * capacity, :] = part.reshape(
                expert_count, capacity, half
            )


def run_expert(order, gate, up, c, wg, wu, wd, expert_count, step_groups):
    groups, rows, feat = c[0].shape
    width, hidden = wg.shape
    pipes = width // feat
    half = feat // 2
    step_rows = step_groups * rows
    step_slots = step_rows // expert_count
    everything = groups * rows
    steps = groups // step_groups
    whole = lambda shape: pl.BlockSpec(shape, lambda s, o: (0, 0))
    flipped = pl.BlockSpec((hidden, step_rows), lambda s, o: (0, s))
    straight = pl.BlockSpec((step_rows, hidden), lambda s, o: (s, 0))
    block = (step_groups, rows, feat)
    piece = pl.BlockSpec(block, lambda s, o: (s, 0, 0))
    return pl.pallas_call(
        functools.partial(expert_kernel, expert_count),
        grid_spec=pltpu.PrefetchScalarGridSpec(
            num_scalar_prefetch=1,
            grid=(steps,),
            in_specs=[
                straight,
                straight,
                piece,
                piece,
                piece,
                pl.BlockSpec(block, lambda s, o: (jnp.minimum(s, steps // 2 - 1), 0, 0)),
                pl.BlockSpec(block, lambda s, o: (jnp.maximum(s - steps // 2, 0), 0, 0)),
                whole((width, hidden)),
                whole((width, hidden)),
                whole((hidden, width)),
            ],
            out_specs=[
                flipped,
                flipped,
                flipped,
                pl.BlockSpec((pipes, step_rows, half), lambda s, o: (0, s, 0)),
                pl.BlockSpec((expert_count, pipes, step_slots, half), lambda s, o: (0, 0, s, 0)),
            ],
        ),
        out_shape=[jax.ShapeDtypeStruct((hidden, everything), BF16)] * 3
        + [
            jax.ShapeDtypeStruct((pipes, everything, half), BF16),
            jax.ShapeDtypeStruct((expert_count, pipes, everything // expert_count, half), BF16),
        ],
        compiler_params=pltpu.CompilerParams(vmem_limit_bytes=58 * MIB),
        name="expert",
        interpret=INTERPRET,
    )(order, gate, up, *c, wg, wu, wd)


def weight_kernel(order_ref, x_ref, c0_ref, c1_ref, c3_ref, c2x_ref, c2y_ref, act_ref, gg_ref, ug_ref, dwg_ref, dwu_ref, dwd_ref):
    groups, _, rows, feat = x_ref.shape
    step = pl.program_id(0)
    features = x_ref[:, 0].reshape(groups * rows, feat)
    dwg_ref[...] = dot(gg_ref[...], features).astype(BF16).T
    dwu_ref[...] = dot(ug_ref[...], features).astype(BF16).T

    def down(value):
        dwd_ref[...] = dot(act_ref[...], value.reshape(groups * rows, feat)).astype(BF16)

    pl.when(step == 0)(lambda: down(c0_ref[...]))
    pl.when(step == 1)(lambda: down(c3_ref[...]))
    pl.when(step == 2)(lambda: down(jnp.concatenate([c2x_ref[...], c2y_ref[...]], axis=0)))
    pl.when(step == 3)(lambda: down(c1_ref[...]))


def run_weights(order, x, c, act, gg, ug):
    groups, pipes, rows, feat = x.shape
    hidden, everything = act.shape
    whole = pl.BlockSpec((hidden, everything), lambda p, o: (0, 0))
    piece = lambda v: pl.BlockSpec(v.shape, lambda p, o: (0, 0, 0))
    return pl.pallas_call(
        weight_kernel,
        grid_spec=pltpu.PrefetchScalarGridSpec(
            num_scalar_prefetch=1,
            grid=(pipes,),
            in_specs=[pl.BlockSpec((groups, 1, rows, feat), lambda p, o: (0, p, 0, 0))]
            + [piece(v) for v in c]
            + [whole] * 3,
            out_specs=[
                pl.BlockSpec((feat, hidden), lambda p, o: (p, 0)),
                pl.BlockSpec((feat, hidden), lambda p, o: (p, 0)),
                pl.BlockSpec((hidden, feat), lambda p, o: (0, o[p])),
            ],
        ),
        out_shape=[
            jax.ShapeDtypeStruct((pipes * feat, hidden), BF16),
            jax.ShapeDtypeStruct((pipes * feat, hidden), BF16),
            jax.ShapeDtypeStruct((hidden, pipes * feat), BF16),
        ],
        compiler_params=pltpu.CompilerParams(vmem_limit_bytes=58 * MIB),
        name="weights",
        interpret=INTERPRET,
    )(order, x, *c, act, gg, ug)


def combine_kernel(x_ref, slots_ref, out_ref):
    experts, pipes, slots, half = x_ref.shape
    group_count, tokens, _ = slots_ref.shape
    capacity = slots // group_count
    want = lax.broadcasted_iota(jnp.int32, (tokens, experts * capacity), 1)
    for d in range(group_count):
        picked = (slots_ref[d, :, 0:1] == want) | (slots_ref[d, :, 1:2] == want)
        chosen = jnp.where(picked, 1.0, 0.0).astype(BF16)
        for p in range(pipes):
            rows = x_ref[:, p, d * capacity : (d + 1) * capacity, :]
            rows = rows.reshape(experts * capacity, half)
            out_ref[p, d * tokens : (d + 1) * tokens, :] = dot(chosen, rows).astype(BF16)


def total_of(parts):
    total = parts[0].astype(F32)
    for k in range(1, parts.shape[0]):
        total = total + parts[k].astype(F32)
    return total.astype(BF16)


def run_combine(x, slots):
    experts, pipes, everything, half = x.shape
    group_count, tokens, _ = slots.shape
    here = pl.BlockSpec(memory_space=pltpu.VMEM)
    return pl.pallas_call(
        combine_kernel,
        in_specs=[here, here],
        out_specs=here,
        out_shape=jax.ShapeDtypeStruct((pipes, group_count * tokens, half), BF16),
        compiler_params=pltpu.CompilerParams(vmem_limit_bytes=10 * MIB),
        name="combine",
        interpret=INTERPRET,
    )(x, slots)


def shift(x, axis, by):
    count = lax.axis_size(axis)
    return lax.ppermute(x, axis, [(k, (k + by) % count) for k in range(count)])


def place_kernel(at_ref, *refs):
    pieces, out_ref = refs[:-1], refs[-1]
    count = out_ref.shape[0]
    cut = pieces[-2].shape[0]
    for j in range(count - 1):
        out_ref[at_ref[j]] = pieces[j][...]
    out_ref[at_ref[count - 1], :cut] = pieces[-2][...]
    out_ref[at_ref[count - 1], cut:] = pieces[-1][...]


def groups_ring(x):
    rows, width = x.shape
    cut = rows // 2
    up1, down1 = shift(x, "dp", 1), shift(x, "dp", -1)
    up2, down2 = shift(up1, "dp", 1), shift(down1, "dp", -1)
    up3, down3 = shift(up2, "dp", 1), shift(down2, "dp", -1)
    far_up, far_down = shift(up3[:cut], "dp", 1), shift(down3[cut:], "dp", -1)
    count = lax.axis_size("dp")
    at = (lax.axis_index("dp") + jnp.array([0, 1, 2, 3, 5, 6, 7, 4], jnp.int32)) % count
    here = pl.BlockSpec(memory_space=pltpu.VMEM)
    return pl.pallas_call(
        place_kernel,
        in_specs=[pl.BlockSpec(memory_space=pltpu.SMEM)] + [here] * (count + 1),
        out_specs=here,
        out_shape=jax.ShapeDtypeStruct((count, rows, width), BF16),
        compiler_params=pltpu.CompilerParams(vmem_limit_bytes=6 * MIB),
        name="place",
        interpret=INTERPRET,
    )(at, x, down1, down2, down3, up3, up2, up1, far_up, far_down)


def pipes_ring(x):
    cut = x.shape[0] // 2
    up1, down1 = shift(x, "pipe", 1), shift(x, "pipe", -1)
    with jax.named_scope("pipe_last"):
        far_up, far_down = shift(up1[:cut], "pipe", 1), shift(down1[cut:], "pipe", -1)
    return x, up1, down1, far_up, far_down


def body(tokens, out_grad, gate_values, expert_ids, w_gate, w_up, w_down):
    expert_count = lax.axis_size("expert")
    group_count = lax.axis_size("dp")
    pipe_count = lax.axis_size("pipe")
    token_count, feat = tokens.shape
    capacity = max(token_count // 2, 2 * token_count // expert_count)
    slot_total = expert_count * capacity
    half = feat // 2
    slot_index = slot_indices(expert_ids, expert_count, capacity)
    picker, sent_rows, sent_grads = fill_slots(
        slot_index, gate_values, slot_total, tokens, out_grad
    )
    sent = jnp.concatenate(
        [
            sent_rows.reshape(expert_count, 1, capacity, feat),
            sent_grads.reshape(expert_count, 1, capacity, feat),
        ],
        axis=1,
    )
    received = lax.all_to_all(sent, "expert", split_axis=0, concat_axis=0, tiled=True)
    x = lax.all_gather(
        received[:, 0].reshape(1, slot_total, feat), ("dp", "pipe"), axis=0, tiled=True
    )
    x = x.reshape(group_count, pipe_count, slot_total, feat)
    c = pipes_ring(groups_ring(received[:, 1].reshape(slot_total, feat)))
    order = (lax.axis_index("pipe") + jnp.arange(pipe_count, dtype=jnp.int32)) % pipe_count
    gate, up = run_project(x, w_gate[0], w_up[0], group_count // 4)
    act, gg, ug, ring, cross = run_expert(
        order, gate, up, c, w_gate[0], w_up[0], w_down[0], expert_count, group_count // 4
    )
    late_index, gg = lax.optimization_barrier((slot_index, gg))
    column_slots = lax.all_gather(late_index[None], "dp", axis=0, tiled=True)
    over_pipe = lax.psum_scatter(ring, "pipe", scatter_dimension=0, tiled=True)
    crossed = lax.all_to_all(cross, "expert", split_axis=0, concat_axis=0, tiled=True)
    gate_weight_gradient, up_weight_gradient, grad_down = run_weights(order, x, c, act, gg, ug)
    over_pipe, column_slots, grad_down = lax.optimization_barrier(
        (over_pipe, column_slots, grad_down)
    )
    summed = lax.psum_scatter(
        over_pipe.reshape(group_count, slot_total, half), "dp", scatter_dimension=0, tiled=True
    )
    column = run_combine(crossed, column_slots)
    column = lax.all_to_all(column, "pipe", split_axis=0, concat_axis=0, tiled=True)
    column = total_of(column)
    column = lax.all_to_all(
        column.reshape(group_count, token_count, half), "dp", split_axis=0, concat_axis=0, tiled=True
    )
    right = total_of(column)
    returned = lax.all_to_all(
        summed.reshape(expert_count, capacity, half), "expert", split_axis=0, concat_axis=0, tiled=True
    )
    left = jnp.einsum(
        "st,sq->tq", picker, returned.reshape(slot_total, half), preferred_element_type=F32
    ).astype(BF16)
    grad_tokens = jnp.concatenate([left, right], axis=1)
    return (
        grad_tokens,
        gate_weight_gradient[None],
        up_weight_gradient[None],
        grad_down[None],
    )


def solution(mesh):
    rows = P(("expert", "dp"), "pipe")
    pairs = P(("expert", "dp"), None)
    wide = P("expert", None, ("dp", "pipe"))
    tall = P("expert", ("dp", "pipe"), None)
    return jax.shard_map(
        body,
        mesh=mesh,
        in_specs=(rows, rows, pairs, pairs, wide, wide, tall),
        out_specs=(rows, wide, wide, tall),
        check_vma=False,
    )
```

```python
import functools

import jax
import jax.numpy as jnp
from jax import lax
from jax.experimental import pallas as pl
from jax.experimental.pallas import tpu as pltpu
from jax.sharding import PartitionSpec as P

F32 = jnp.float32
BF16 = jnp.bfloat16
INTERPRET = False
MIB = 1024 * 1024
NN = (((1,), (0,)), ((), ()))
NT = (((1,), (1,)), ((), ()))


def dot(a, b, dims=NN):
    return lax.dot_general(a, b, dims, preferred_element_type=F32)


def dispatch_kernel(expert_count, ids_ref, gates_ref, g_ref, *refs):
    pieces, (sent_ref, slots_ref, picker_ref) = refs[:-3], refs[-3:]
    tokens, feat = g_ref.shape
    capacity = sent_ref.shape[2]
    first, second = ids_ref[0:1, :], ids_ref[1:2, :]
    row = lax.broadcasted_iota(jnp.int32, (tokens, tokens), 0)
    col = lax.broadcasted_iota(jnp.int32, (tokens, tokens), 1)
    tall_first = jnp.sum(jnp.where(row == col, first, 0), axis=1, keepdims=True)
    tall_second = jnp.sum(jnp.where(row == col, second, 0), axis=1, keepdims=True)

    def slot_of(ids):
        same = (tall_first == ids).astype(jnp.int32) + (tall_second == ids).astype(jnp.int32)
        rank = jnp.sum(jnp.where(row < col, same, 0), axis=0, keepdims=True)
        return ids * capacity + rank

    slot_first, slot_second = slot_of(first), slot_of(second)
    slots_ref[0:1, :] = slot_first
    slots_ref[1:2, :] = slot_second
    want = lax.broadcasted_iota(jnp.int32, (expert_count * capacity, tokens), 0)
    hit_first, hit_second = slot_first == want, slot_second == want
    picker = jnp.where(hit_first | hit_second, 1.0, 0.0).astype(BF16)
    picker_ref[...] = picker
    gates = jnp.where(hit_first, gates_ref[0:1, :], 0.0) + jnp.where(
        hit_second, gates_ref[1:2, :], 0.0
    )
    gate = jnp.sum(gates, axis=1, keepdims=True)
    for k, piece in enumerate(pieces):
        rows = dot(picker, piece[...]).astype(BF16)
        sent_ref[:, k] = rows.reshape(expert_count, capacity, feat)
    scaled = (gate * dot(picker, g_ref[...])).astype(BF16)
    sent_ref[:, len(pieces)] = scaled.reshape(expert_count, capacity, feat)


def run_dispatch(ids, gates, out_grad, pieces, expert_count, capacity):
    tokens, feat = out_grad.shape
    here = pl.BlockSpec(memory_space=pltpu.VMEM)
    return pl.pallas_call(
        functools.partial(dispatch_kernel, expert_count),
        in_specs=[here] * (3 + len(pieces)),
        out_specs=[here] * 3,
        out_shape=[
            jax.ShapeDtypeStruct((expert_count, len(pieces) + 1, capacity, feat), BF16),
            jax.ShapeDtypeStruct((2, tokens), jnp.int32),
            jax.ShapeDtypeStruct((expert_count * capacity, tokens), BF16),
        ],
        compiler_params=pltpu.CompilerParams(vmem_limit_bytes=8 * MIB),
        name="dispatch",
        interpret=INTERPRET,
    )(ids, gates, out_grad, *pieces)


def project_kernel(order_ref, x_ref, wg_ref, wu_ref, gate_ref, up_ref):
    groups, pipes, rows, feat = x_ref.shape
    total = groups * rows
    gate = up = None
    for p in range(pipes):
        features = x_ref[:, p].reshape(total, feat)
        cols = pl.ds(pl.multiple_of(order_ref[p] * feat, 128), feat)
        g = dot(features, wg_ref[cols, :])
        u = dot(features, wu_ref[cols, :])
        gate = g if gate is None else gate + g
        up = u if up is None else up + u
    gate_ref[...] = gate
    up_ref[...] = up


def run_project(order, x, wg, wu, step_groups):
    groups, pipes, rows, feat = x.shape
    width, hidden = wg.shape
    step_rows = step_groups * rows
    whole = pl.BlockSpec((width, hidden), lambda s, o: (0, 0))
    result = pl.BlockSpec((step_rows, hidden), lambda s, o: (s, 0))
    return pl.pallas_call(
        project_kernel,
        grid_spec=pltpu.PrefetchScalarGridSpec(
            num_scalar_prefetch=1,
            grid=(groups // step_groups,),
            in_specs=[
                pl.BlockSpec((step_groups, pipes, rows, feat), lambda s, o: (s, 0, 0, 0)),
                whole,
                whole,
            ],
            out_specs=[result, result],
        ),
        out_shape=[jax.ShapeDtypeStruct((groups * rows, hidden), F32)] * 2,
        compiler_params=pltpu.CompilerParams(vmem_limit_bytes=58 * MIB),
        name="project",
        interpret=INTERPRET,
    )(order, x, wg, wu)


def expert_kernel(expert_count, order_ref, gate_ref, up_ref, c0_ref, c1_ref, c3_ref, c2x_ref, c2y_ref, wg_ref, wu_ref, wd_ref, act_ref, gg_ref, ug_ref, ring_ref, cross_ref):
    groups, rows, feat = c0_ref.shape
    pipes = wg_ref.shape[0] // feat
    total = groups * rows
    half = feat // 2
    capacity = rows // expert_count
    early = pl.program_id(0) < pl.num_programs(0) // 2
    opposite = jnp.where(early, c2x_ref[...], c2y_ref[...])
    act_grad = None
    for k, value in enumerate((c0_ref[...], c3_ref[...], opposite, c1_ref[...])):
        cols = pl.ds(pl.multiple_of(order_ref[k] * feat, 128), feat)
        a = dot(value.reshape(total, feat), wd_ref[:, cols], NT)
        act_grad = a if act_grad is None else act_grad + a
    gate = gate_ref[...]
    up = up_ref[...]
    sig = jax.nn.sigmoid(gate)
    linear = gate * sig
    act = (linear * up).astype(BF16)
    gate_grad = (act_grad * up * (sig * (1.0 + gate * (1.0 - sig)))).astype(BF16)
    up_grad = (act_grad * linear).astype(BF16)
    act_ref[...] = act.T
    gg_ref[...] = gate_grad.T
    ug_ref[...] = up_grad.T
    for p in range(pipes):
        cols = slice(p * feat, (p + 1) * feat)
        back = (dot(gate_grad, wg_ref[cols, :], NT) + dot(up_grad, wu_ref[cols, :], NT)).astype(BF16)
        for d in range(groups):
            ring_ref[d, p] = back[d * rows : (d + 1) * rows, :half]
            part = back[d * rows : (d + 1) * rows, half:]
            cross_ref[:, p, d * capacity : (d + 1) * capacity, :] = part.reshape(
                expert_count, capacity, half
            )


def run_expert(order, gate, up, c, wg, wu, wd, expert_count, step_groups):
    groups, rows, feat = c[0].shape
    width, hidden = wg.shape
    pipes = width // feat
    half = feat // 2
    step_rows = step_groups * rows
    step_slots = step_rows // expert_count
    everything = groups * rows
    steps = groups // step_groups
    whole = lambda shape: pl.BlockSpec(shape, lambda s, o: (0, 0))
    flipped = pl.BlockSpec((hidden, step_rows), lambda s, o: (0, s))
    straight = pl.BlockSpec((step_rows, hidden), lambda s, o: (s, 0))
    block = (step_groups, rows, feat)
    piece = pl.BlockSpec(block, lambda s, o: (s, 0, 0))
    return pl.pallas_call(
        functools.partial(expert_kernel, expert_count),
        grid_spec=pltpu.PrefetchScalarGridSpec(
            num_scalar_prefetch=1,
            grid=(steps,),
            in_specs=[
                straight,
                straight,
                piece,
                piece,
                piece,
                pl.BlockSpec(block, lambda s, o: (jnp.minimum(s, steps // 2 - 1), 0, 0)),
                pl.BlockSpec(block, lambda s, o: (jnp.maximum(s - steps // 2, 0), 0, 0)),
                whole((width, hidden)),
                whole((width, hidden)),
                whole((hidden, width)),
            ],
            out_specs=[
                flipped,
                flipped,
                flipped,
                pl.BlockSpec((step_groups, pipes, rows, half), lambda s, o: (s, 0, 0, 0)),
                pl.BlockSpec((expert_count, pipes, step_slots, half), lambda s, o: (0, 0, s, 0)),
            ],
        ),
        out_shape=[jax.ShapeDtypeStruct((hidden, everything), BF16)] * 3
        + [
            jax.ShapeDtypeStruct((groups, pipes, rows, half), BF16),
            jax.ShapeDtypeStruct((expert_count, pipes, everything // expert_count, half), BF16),
        ],
        compiler_params=pltpu.CompilerParams(vmem_limit_bytes=58 * MIB),
        name="expert",
        interpret=INTERPRET,
    )(order, gate, up, *c, wg, wu, wd)


def weight_kernel(order_ref, x_ref, c0_ref, c1_ref, c3_ref, c2x_ref, c2y_ref, act_ref, gg_ref, ug_ref, dwg_ref, dwu_ref, dwd_ref):
    groups, _, rows, feat = x_ref.shape
    step = pl.program_id(0)
    features = x_ref[:, 0].reshape(groups * rows, feat)
    dwg_ref[...] = dot(gg_ref[...], features).astype(BF16).T
    dwu_ref[...] = dot(ug_ref[...], features).astype(BF16).T

    def down(value):
        dwd_ref[...] = dot(act_ref[...], value.reshape(groups * rows, feat)).astype(BF16)

    pl.when(step == 0)(lambda: down(c0_ref[...]))
    pl.when(step == 1)(lambda: down(c3_ref[...]))
    pl.when(step == 2)(lambda: down(jnp.concatenate([c2x_ref[...], c2y_ref[...]], axis=0)))
    pl.when(step == 3)(lambda: down(c1_ref[...]))


def run_weights(order, x, c, act, gg, ug):
    groups, pipes, rows, feat = x.shape
    hidden, everything = act.shape
    whole = pl.BlockSpec((hidden, everything), lambda p, o: (0, 0))
    piece = lambda v: pl.BlockSpec(v.shape, lambda p, o: (0, 0, 0))
    return pl.pallas_call(
        weight_kernel,
        grid_spec=pltpu.PrefetchScalarGridSpec(
            num_scalar_prefetch=1,
            grid=(pipes,),
            in_specs=[pl.BlockSpec((groups, 1, rows, feat), lambda p, o: (0, p, 0, 0))]
            + [piece(v) for v in c]
            + [whole] * 3,
            out_specs=[
                pl.BlockSpec((feat, hidden), lambda p, o: (o[p], 0)),
                pl.BlockSpec((feat, hidden), lambda p, o: (o[p], 0)),
                pl.BlockSpec((hidden, feat), lambda p, o: (0, o[p])),
            ],
        ),
        out_shape=[
            jax.ShapeDtypeStruct((pipes * feat, hidden), BF16),
            jax.ShapeDtypeStruct((pipes * feat, hidden), BF16),
            jax.ShapeDtypeStruct((hidden, pipes * feat), BF16),
        ],
        compiler_params=pltpu.CompilerParams(vmem_limit_bytes=58 * MIB),
        name="weights",
        interpret=INTERPRET,
    )(order, x, *c, act, gg, ug)


def combine_kernel(x_ref, slots_ref, out_ref):
    experts, pipes, slots, half = x_ref.shape
    group_count, _, tokens = slots_ref.shape
    capacity = slots // group_count
    want = lax.broadcasted_iota(jnp.int32, (experts * capacity, tokens), 0)
    for d in range(group_count):
        picked = (slots_ref[d, 0:1, :] == want) | (slots_ref[d, 1:2, :] == want)
        chosen = jnp.where(picked, 1.0, 0.0).astype(BF16)
        for p in range(pipes):
            rows = x_ref[:, p, d * capacity : (d + 1) * capacity, :]
            rows = rows.reshape(experts * capacity, half)
            out_ref[p, d * tokens : (d + 1) * tokens, :] = dot(
                chosen, rows, (((0,), (0,)), ((), ()))
            ).astype(BF16)


def total_of(parts):
    total = parts[0].astype(F32)
    for k in range(1, parts.shape[0]):
        total = total + parts[k].astype(F32)
    return total.astype(BF16)


def run_combine(x, slots):
    _, pipes, _, half = x.shape
    group_count, _, tokens = slots.shape
    here = pl.BlockSpec(memory_space=pltpu.VMEM)
    return pl.pallas_call(
        combine_kernel,
        in_specs=[here, here],
        out_specs=here,
        out_shape=jax.ShapeDtypeStruct((pipes, group_count * tokens, half), BF16),
        compiler_params=pltpu.CompilerParams(vmem_limit_bytes=10 * MIB),
        name="combine",
        interpret=INTERPRET,
    )(x, slots)


def shift(x, axis, by):
    count = lax.axis_size(axis)
    return lax.ppermute(x, axis, [(k, (k + by) % count) for k in range(count)])


def place_kernel(at_ref, *refs):
    pieces, out_ref = refs[:-1], refs[-1]
    count = out_ref.shape[0]
    cut = pieces[-2].shape[0]
    for j in range(count - 1):
        out_ref[at_ref[j]] = pieces[j][...]
    out_ref[at_ref[count - 1], :cut] = pieces[-2][...]
    out_ref[at_ref[count - 1], cut:] = pieces[-1][...]


def groups_ring(x):
    rows, width = x.shape
    cut = rows // 2
    up1, down1 = shift(x, "dp", 1), shift(x, "dp", -1)
    up2, down2 = shift(up1, "dp", 1), shift(down1, "dp", -1)
    up3, down3 = shift(up2, "dp", 1), shift(down2, "dp", -1)
    far_up, far_down = shift(up3[:cut], "dp", 1), shift(down3[cut:], "dp", -1)
    count = lax.axis_size("dp")
    at = (lax.axis_index("dp") + jnp.array([0, 1, 2, 3, 5, 6, 7, 4], jnp.int32)) % count
    here = pl.BlockSpec(memory_space=pltpu.VMEM)
    return pl.pallas_call(
        place_kernel,
        in_specs=[pl.BlockSpec(memory_space=pltpu.SMEM)] + [here] * (count + 1),
        out_specs=here,
        out_shape=jax.ShapeDtypeStruct((count, rows, width), BF16),
        compiler_params=pltpu.CompilerParams(vmem_limit_bytes=6 * MIB),
        name="place",
        interpret=INTERPRET,
    )(at, x, down1, down2, down3, up3, up2, up1, far_up, far_down)


def pipes_ring(x):
    cut = x.shape[0] // 2
    up1, down1 = shift(x, "pipe", 1), shift(x, "pipe", -1)
    far_up, far_down = shift(up1[:cut], "pipe", 1), shift(down1[cut:], "pipe", -1)
    return x, up1, down1, far_up, far_down


def body(tokens, out_grad, gate_values, expert_ids, w_gate, w_up, w_down):
    expert_count = lax.axis_size("expert")
    group_count = lax.axis_size("dp")
    pipe_count = lax.axis_size("pipe")
    token_count, feat = tokens.shape
    capacity = max(token_count // 2, 2 * token_count // expert_count)
    slot_total = expert_count * capacity
    half = feat // 2
    pieces = (tokens, shift(tokens, "pipe", -1), shift(tokens, "pipe", 2), shift(tokens, "pipe", 1))
    sent, slot_index, picker = run_dispatch(
        expert_ids.T, gate_values.T, out_grad, pieces, expert_count, capacity
    )
    received = lax.all_to_all(sent, "expert", split_axis=0, concat_axis=0, tiled=True)
    near = received[:, :pipe_count].transpose(1, 0, 2, 3).reshape(1, pipe_count, slot_total, feat)
    x = lax.all_gather(near, "dp", axis=0, tiled=True)
    c = pipes_ring(groups_ring(received[:, pipe_count].reshape(slot_total, feat)))
    order = (lax.axis_index("pipe") + jnp.arange(pipe_count, dtype=jnp.int32)) % pipe_count
    gate, up = run_project(order, x, w_gate[0], w_up[0], group_count // 4)
    act, gg, ug, ring, cross = run_expert(
        order, gate, up, c, w_gate[0], w_up[0], w_down[0], expert_count, group_count // 4
    )
    over_groups = lax.psum_scatter(
        ring.reshape(group_count, pipe_count * slot_total, half), "dp", scatter_dimension=0, tiled=True
    )
    crossed = lax.all_to_all(cross, "expert", split_axis=0, concat_axis=0, tiled=True)
    late_index, gg = lax.optimization_barrier((slot_index, gg))
    column_slots = lax.all_gather(late_index[None], "dp", axis=0, tiled=True)
    gate_weight_gradient, up_weight_gradient, grad_down = run_weights(order, x, c, act, gg, ug)
    over_groups, column_slots, grad_down = lax.optimization_barrier(
        (over_groups, column_slots, grad_down)
    )
    summed = lax.psum_scatter(
        over_groups.reshape(pipe_count, slot_total, half), "pipe", scatter_dimension=0, tiled=True
    )
    column = run_combine(crossed, column_slots)
    column = lax.all_to_all(column, "pipe", split_axis=0, concat_axis=0, tiled=True)
    column = total_of(column)
    column = lax.all_to_all(
        column.reshape(group_count, token_count, half),
        "dp",
        split_axis=0,
        concat_axis=0,
        tiled=True,
    )
    right = total_of(column)
    returned = lax.all_to_all(
        summed.reshape(expert_count, capacity, half),
        "expert",
        split_axis=0,
        concat_axis=0,
        tiled=True,
    )
    left = jnp.einsum(
        "st,sq->tq", picker, returned.reshape(slot_total, half), preferred_element_type=F32
    ).astype(BF16)
    grad_tokens = jnp.concatenate([left, right], axis=1)
    return (
        grad_tokens,
        gate_weight_gradient[None],
        up_weight_gradient[None],
        grad_down[None],
    )


def solution(mesh):
    rows = P(("expert", "dp"), "pipe")
    pairs = P(("expert", "dp"), None)
    wide = P("expert", None, ("dp", "pipe"))
    tall = P("expert", ("dp", "pipe"), None)

    return jax.shard_map(
        body,
        mesh=mesh,
        in_specs=(rows, rows, pairs, pairs, wide, wide, tall),
        out_specs=(rows, wide, wide, tall),
        check_vma=False,
    )
```

```python
import functools

import jax
import jax.numpy as jnp
from jax import lax
from jax.experimental import pallas as pl
from jax.experimental.pallas import tpu as pltpu
from jax.sharding import PartitionSpec as P


F32 = jnp.float32
BF16 = jnp.bfloat16
INTERPRET = False
MIB = 1024 * 1024
NN = (((1,), (0,)), ((), ()))
NT = (((1,), (1,)), ((), ()))
TN = (((0,), (0,)), ((), ()))


def dot(a, b, dims=NN):
    return lax.dot_general(a, b, dims, preferred_element_type=F32)


def dispatch_kernel(expert_count, ids_ref, gates_ref, g_ref, *refs):
    pieces, (sent_ref, slots_ref, picker_ref) = refs[:-3], refs[-3:]
    tokens, feat = g_ref.shape
    capacity = sent_ref.shape[2]
    first, second = ids_ref[0:1, :], ids_ref[1:2, :]
    row = lax.broadcasted_iota(jnp.int32, (tokens, tokens), 0)
    col = lax.broadcasted_iota(jnp.int32, (tokens, tokens), 1)
    tall_first = jnp.sum(jnp.where(row == col, first, 0), axis=1, keepdims=True)
    tall_second = jnp.sum(jnp.where(row == col, second, 0), axis=1, keepdims=True)

    def slot_of(ids):
        same = (tall_first == ids).astype(jnp.int32) + (tall_second == ids).astype(jnp.int32)
        rank = jnp.sum(jnp.where(row < col, same, 0), axis=0, keepdims=True)
        return ids * capacity + rank

    slot_first, slot_second = slot_of(first), slot_of(second)
    slots_ref[0:1, :] = slot_first
    slots_ref[1:2, :] = slot_second
    want = lax.broadcasted_iota(jnp.int32, (expert_count * capacity, tokens), 0)
    hit_first, hit_second = slot_first == want, slot_second == want
    picker = jnp.where(hit_first | hit_second, 1.0, 0.0).astype(BF16)
    picker_ref[...] = picker
    gates = jnp.where(hit_first, gates_ref[0:1, :], 0.0) + jnp.where(
        hit_second, gates_ref[1:2, :], 0.0
    )
    gate = jnp.sum(gates, axis=1, keepdims=True)
    for k, piece in enumerate(pieces):
        rows = dot(picker, piece[...]).astype(BF16)
        sent_ref[:, k] = rows.reshape(expert_count, capacity, feat)
    scaled = (gate * dot(picker, g_ref[...])).astype(BF16)
    sent_ref[:, len(pieces)] = scaled.reshape(expert_count, capacity, feat)


def run_dispatch(ids, gates, out_grad, pieces, expert_count, capacity):
    tokens, feat = out_grad.shape
    here = pl.BlockSpec(memory_space=pltpu.VMEM)
    return pl.pallas_call(
        functools.partial(dispatch_kernel, expert_count),
        in_specs=[here] * (3 + len(pieces)),
        out_specs=[here] * 3,
        out_shape=[
            jax.ShapeDtypeStruct((expert_count, len(pieces) + 1, capacity, feat), BF16),
            jax.ShapeDtypeStruct((2, tokens), jnp.int32),
            jax.ShapeDtypeStruct((expert_count * capacity, tokens), BF16),
        ],
        compiler_params=pltpu.CompilerParams(vmem_limit_bytes=58 * MIB),
        name="dispatch",
        interpret=INTERPRET,
    )(ids, gates, out_grad, *pieces)


def in_order(pieces, early):
    own, before, after, far_early, far_late = pieces
    return own[...], after[...], jnp.where(early, far_early[...], far_late[...]), before[...]


def project_kernel(order_ref, *refs):
    pieces, (wg_ref, wu_ref, gate_ref, up_ref) = refs[:5], refs[5:]
    groups, rows, feat = pieces[0].shape
    early = pl.program_id(0) < pl.num_programs(0) // 2
    gate = up = None
    for k, value in enumerate(in_order(pieces, early)):
        features = value.reshape(groups * rows, feat)
        cols = pl.ds(pl.multiple_of(order_ref[k] * feat, 128), feat)
        g = dot(features, wg_ref[cols, :])
        u = dot(features, wu_ref[cols, :])
        gate = g if gate is None else gate + g
        up = u if up is None else up + u
    gate_ref[...] = gate
    up_ref[...] = up


def run_project(order, c, wg, wu, step_groups):
    groups, rows, feat = c[0].shape
    width, hidden = wg.shape
    steps = groups // step_groups
    step_rows = step_groups * rows
    block = (step_groups, rows, feat)
    piece = pl.BlockSpec(block, lambda s, o: (s, 0, 0))
    whole = pl.BlockSpec((width, hidden), lambda s, o: (0, 0))
    result = pl.BlockSpec((step_rows, hidden), lambda s, o: (s, 0))
    return pl.pallas_call(
        project_kernel,
        grid_spec=pltpu.PrefetchScalarGridSpec(
            num_scalar_prefetch=1,
            grid=(steps,),
            in_specs=[
                piece,
                piece,
                piece,
                pl.BlockSpec(block, lambda s, o: (jnp.minimum(s, steps // 2 - 1), 0, 0)),
                pl.BlockSpec(block, lambda s, o: (jnp.maximum(s - steps // 2, 0), 0, 0)),
                whole,
                whole,
            ],
            out_specs=[result, result],
        ),
        out_shape=[jax.ShapeDtypeStruct((groups * rows, hidden), F32)] * 2,
        compiler_params=pltpu.CompilerParams(vmem_limit_bytes=58 * MIB),
        name="project",
        interpret=INTERPRET,
    )(order, *c, wg, wu)


def expert_kernel(expert_count, order_ref, gate_ref, up_ref, x_ref, wg_ref, wu_ref, wd_ref, act_ref, gg_ref, ug_ref, ring_ref, cross_ref):
    groups, pipes, rows, feat = x_ref.shape
    total = groups * rows
    half = feat // 2
    capacity = rows // expert_count
    act_grad = None
    for k in range(pipes):
        cols = pl.ds(pl.multiple_of(order_ref[k] * feat, 128), feat)
        a = dot(x_ref[:, k].reshape(total, feat), wd_ref[:, cols], NT)
        act_grad = a if act_grad is None else act_grad + a
    gate = gate_ref[...]
    up = up_ref[...]
    sig = jax.nn.sigmoid(gate)
    linear = gate * sig
    gate_grad = (act_grad * up * (sig * (1.0 + gate * (1.0 - sig)))).astype(BF16)
    up_grad = (act_grad * linear).astype(BF16)
    act_ref[...] = (linear * up).astype(BF16)
    gg_ref[...] = gate_grad
    ug_ref[...] = up_grad
    for p in range(pipes):
        cols = slice(p * feat, (p + 1) * feat)
        back = (dot(gate_grad, wg_ref[cols, :], NT) + dot(up_grad, wu_ref[cols, :], NT)).astype(BF16)
        for d in range(groups):
            ring_ref[d, p] = back[d * rows : (d + 1) * rows, :half]
            part = back[d * rows : (d + 1) * rows, half:]
            cross_ref[:, p, d * capacity : (d + 1) * capacity, :] = part.reshape(
                expert_count, capacity, half
            )


def run_expert(order, gate, up, x, wg, wu, wd, expert_count, step_groups):
    groups, pipes, rows, feat = x.shape
    width, hidden = wg.shape
    half = feat // 2
    step_rows = step_groups * rows
    step_slots = step_rows // expert_count
    everything = groups * rows
    whole = lambda shape: pl.BlockSpec(shape, lambda s, o: (0, 0))
    straight = pl.BlockSpec((step_rows, hidden), lambda s, o: (s, 0))
    return pl.pallas_call(
        functools.partial(expert_kernel, expert_count),
        grid_spec=pltpu.PrefetchScalarGridSpec(
            num_scalar_prefetch=1,
            grid=(groups // step_groups,),
            in_specs=[
                straight,
                straight,
                pl.BlockSpec((step_groups, pipes, rows, feat), lambda s, o: (s, 0, 0, 0)),
                whole((width, hidden)),
                whole((width, hidden)),
                whole((hidden, width)),
            ],
            out_specs=[
                straight,
                straight,
                straight,
                pl.BlockSpec((step_groups, pipes, rows, half), lambda s, o: (s, 0, 0, 0)),
                pl.BlockSpec((expert_count, pipes, step_slots, half), lambda s, o: (0, 0, s, 0)),
            ],
        ),
        out_shape=[jax.ShapeDtypeStruct((everything, hidden), BF16)] * 3
        + [
            jax.ShapeDtypeStruct((groups, pipes, rows, half), BF16),
            jax.ShapeDtypeStruct((expert_count, pipes, everything // expert_count, half), BF16),
        ],
        compiler_params=pltpu.CompilerParams(vmem_limit_bytes=58 * MIB),
        name="expert",
        interpret=INTERPRET,
    )(order, gate, up, x, wg, wu, wd)


def weight_kernel(order_ref, x_ref, own_ref, before_ref, after_ref, early_ref, late_ref, act_ref, gg_ref, ug_ref, dwg_ref, dwu_ref, dwd_ref):
    groups, _, rows, feat = x_ref.shape
    step = pl.program_id(0)
    cotangent = x_ref[:, 0].reshape(groups * rows, feat)
    dwd_ref[...] = dot(act_ref[...], cotangent, TN).astype(BF16)

    def wide(value):
        features = value.reshape(groups * rows, feat)
        dwg_ref[...] = dot(gg_ref[...], features, TN).astype(BF16).T
        dwu_ref[...] = dot(ug_ref[...], features, TN).astype(BF16).T

    pl.when(step == 0)(lambda: wide(own_ref[...]))
    pl.when(step == 1)(lambda: wide(after_ref[...]))
    pl.when(step == 2)(lambda: wide(jnp.concatenate([early_ref[...], late_ref[...]], axis=0)))
    pl.when(step == 3)(lambda: wide(before_ref[...]))


def run_weights(order, x, c, act, gg, ug):
    groups, pipes, rows, feat = x.shape
    everything, hidden = act.shape
    whole = pl.BlockSpec((everything, hidden), lambda p, o: (0, 0))
    piece = lambda v: pl.BlockSpec(v.shape, lambda p, o: (0, 0, 0))
    return pl.pallas_call(
        weight_kernel,
        grid_spec=pltpu.PrefetchScalarGridSpec(
            num_scalar_prefetch=1,
            grid=(pipes,),
            in_specs=[pl.BlockSpec((groups, 1, rows, feat), lambda p, o: (0, p, 0, 0))]
            + [piece(v) for v in c]
            + [whole] * 3,
            out_specs=[
                pl.BlockSpec((feat, hidden), lambda p, o: (o[p], 0)),
                pl.BlockSpec((feat, hidden), lambda p, o: (o[p], 0)),
                pl.BlockSpec((hidden, feat), lambda p, o: (0, o[p])),
            ],
        ),
        out_shape=[
            jax.ShapeDtypeStruct((pipes * feat, hidden), BF16),
            jax.ShapeDtypeStruct((pipes * feat, hidden), BF16),
            jax.ShapeDtypeStruct((hidden, pipes * feat), BF16),
        ],
        compiler_params=pltpu.CompilerParams(vmem_limit_bytes=58 * MIB),
        name="weights",
        interpret=INTERPRET,
    )(order, x, *c, act, gg, ug)


def combine_kernel(x_ref, slots_ref, out_ref):
    experts, pipes, slots, half = x_ref.shape
    group_count, _, tokens = slots_ref.shape
    capacity = slots // group_count
    want = lax.broadcasted_iota(jnp.int32, (experts * capacity, tokens), 0)
    for d in range(group_count):
        picked = (slots_ref[d, 0:1, :] == want) | (slots_ref[d, 1:2, :] == want)
        chosen = jnp.where(picked, 1.0, 0.0).astype(BF16)
        for p in range(pipes):
            rows = x_ref[:, p, d * capacity : (d + 1) * capacity, :]
            rows = rows.reshape(experts * capacity, half)
            out_ref[p, d * tokens : (d + 1) * tokens, :] = dot(
                chosen, rows, (((0,), (0,)), ((), ()))
            ).astype(BF16)


def total_of(parts):
    total = parts[0].astype(F32)
    for k in range(1, parts.shape[0]):
        total = total + parts[k].astype(F32)
    return total.astype(BF16)


def run_combine(x, slots):
    _, pipes, _, half = x.shape
    group_count, _, tokens = slots.shape
    here = pl.BlockSpec(memory_space=pltpu.VMEM)
    return pl.pallas_call(
        combine_kernel,
        in_specs=[here, here],
        out_specs=here,
        out_shape=jax.ShapeDtypeStruct((pipes, group_count * tokens, half), BF16),
        compiler_params=pltpu.CompilerParams(vmem_limit_bytes=10 * MIB),
        name="combine",
        interpret=INTERPRET,
    )(x, slots)


def shift(x, axis, by):
    count = lax.axis_size(axis)
    return lax.ppermute(x, axis, [(k, (k + by) % count) for k in range(count)])


def place_kernel(at_ref, *refs):
    pieces, out_ref = refs[:-1], refs[-1]
    count = out_ref.shape[0]
    cut = pieces[-2].shape[0]
    for j in range(count - 1):
        out_ref[at_ref[j]] = pieces[j][...]
    out_ref[at_ref[count - 1], :cut] = pieces[-2][...]
    out_ref[at_ref[count - 1], cut:] = pieces[-1][...]


def groups_ring(x):
    rows, width = x.shape
    cut = rows // 2
    up1, down1 = shift(x, "dp", 1), shift(x, "dp", -1)
    up2, down2 = shift(up1, "dp", 1), shift(down1, "dp", -1)
    up3, down3 = shift(up2, "dp", 1), shift(down2, "dp", -1)
    far_up, far_down = shift(up3[:cut], "dp", 1), shift(down3[cut:], "dp", -1)
    count = lax.axis_size("dp")
    at = (lax.axis_index("dp") + jnp.array([0, 1, 2, 3, 5, 6, 7, 4], jnp.int32)) % count
    here = pl.BlockSpec(memory_space=pltpu.VMEM)
    return pl.pallas_call(
        place_kernel,
        in_specs=[pl.BlockSpec(memory_space=pltpu.SMEM)] + [here] * (count + 1),
        out_specs=here,
        out_shape=jax.ShapeDtypeStruct((count, rows, width), BF16),
        compiler_params=pltpu.CompilerParams(vmem_limit_bytes=6 * MIB),
        name="place",
        interpret=INTERPRET,
    )(at, x, down1, down2, down3, up3, up2, up1, far_up, far_down)


def stack_kernel(*refs):
    for k, piece in enumerate(refs[:-1]):
        refs[-1][k] = piece[...]


def run_stack(pieces):
    here = pl.BlockSpec(memory_space=pltpu.VMEM)
    return pl.pallas_call(
        stack_kernel,
        in_specs=[here] * len(pieces),
        out_specs=here,
        out_shape=jax.ShapeDtypeStruct((len(pieces),) + pieces[0].shape, BF16),
        compiler_params=pltpu.CompilerParams(vmem_limit_bytes=6 * MIB),
        name="stack",
        interpret=INTERPRET,
    )(*pieces)


def pipes_ring(x):
    cut = x.shape[0] // 2
    up1, down1 = shift(x, "pipe", 1), shift(x, "pipe", -1)
    far_up, far_down = shift(up1[:cut], "pipe", 1), shift(down1[cut:], "pipe", -1)
    return x, up1, down1, far_up, far_down


def body(tokens, out_grad, gate_values, expert_ids, w_gate, w_up, w_down):
    expert_count = lax.axis_size("expert")
    group_count = lax.axis_size("dp")
    pipe_count = lax.axis_size("pipe")
    token_count, feat = tokens.shape
    capacity = max(token_count // 2, 2 * token_count // expert_count)
    slot_total = expert_count * capacity
    half = feat // 2
    sent, slot_index, picker = run_dispatch(
        expert_ids.T, gate_values.T, out_grad, (tokens,), expert_count, capacity
    )
    received = lax.all_to_all(sent, "expert", split_axis=0, concat_axis=0, tiled=True)
    c = pipes_ring(groups_ring(received[:, 0].reshape(slot_total, feat)))
    own = received[:, 1].reshape(slot_total, feat)
    near = (own, shift(own, "pipe", -1), shift(own, "pipe", 2), shift(own, "pipe", 1))
    near = run_stack(near)
    x = lax.all_gather(near[None], "dp", axis=0, tiled=True)
    order = (lax.axis_index("pipe") + jnp.arange(pipe_count, dtype=jnp.int32)) % pipe_count
    gate, up = run_project(order, c, w_gate[0], w_up[0], group_count // 4)
    act, gg, ug, ring, cross = run_expert(
        order, gate, up, x, w_gate[0], w_up[0], w_down[0], expert_count, group_count // 4
    )
    over_groups = lax.psum_scatter(
        ring.reshape(group_count, pipe_count * slot_total, half), "dp", scatter_dimension=0, tiled=True
    )
    crossed = lax.all_to_all(cross, "expert", split_axis=0, concat_axis=0, tiled=True)
    late_index, gg = lax.optimization_barrier((slot_index, gg))
    column_slots = lax.all_gather(late_index[None], "dp", axis=0, tiled=True)
    gate_weight_gradient, up_weight_gradient, grad_down = run_weights(order, x, c, act, gg, ug)
    over_groups, column_slots, grad_down = lax.optimization_barrier(
        (over_groups, column_slots, grad_down)
    )
    summed = lax.psum_scatter(
        over_groups.reshape(pipe_count, slot_total, half), "pipe", scatter_dimension=0, tiled=True
    )
    column = run_combine(crossed, column_slots)
    column = lax.all_to_all(column, "pipe", split_axis=0, concat_axis=0, tiled=True)
    column = total_of(column)
    column = lax.all_to_all(
        column.reshape(group_count, token_count, half),
        "dp",
        split_axis=0,
        concat_axis=0,
        tiled=True,
    )
    right = total_of(column)
    returned = lax.all_to_all(
        summed.reshape(expert_count, capacity, half),
        "expert",
        split_axis=0,
        concat_axis=0,
        tiled=True,
    )
    left = jnp.einsum(
        "st,sq->tq", picker, returned.reshape(slot_total, half), preferred_element_type=F32
    ).astype(BF16)
    grad_tokens = jnp.concatenate([left, right], axis=1)
    return (
        grad_tokens,
        gate_weight_gradient[None],
        up_weight_gradient[None],
        grad_down[None],
    )


def solution(mesh):
    rows = P(("expert", "dp"), "pipe")
    pairs = P(("expert", "dp"), None)
    wide = P("expert", None, ("dp", "pipe"))
    tall = P("expert", ("dp", "pipe"), None)

    return jax.shard_map(
        body,
        mesh=mesh,
        in_specs=(rows, rows, pairs, pairs, wide, wide, tall),
        out_specs=(rows, wide, wide, tall),
        check_vma=False,
    )
```

```python
import functools

import jax
import jax.numpy as jnp
from jax import lax
from jax.experimental import pallas as pl
from jax.experimental.pallas import tpu as pltpu
from jax.sharding import PartitionSpec as P


F32 = jnp.float32
BF16 = jnp.bfloat16
INTERPRET = False
MIB = 1024 * 1024
NN = (((1,), (0,)), ((), ()))
NT = (((1,), (1,)), ((), ()))
TN = (((0,), (0,)), ((), ()))


def dot(a, b, dims=NN):
    return lax.dot_general(a, b, dims, preferred_element_type=F32)


def dispatch_kernel(expert_count, ids_ref, gates_ref, g_ref, *refs):
    pieces, (sent_ref, slots_ref, picker_ref) = refs[:-3], refs[-3:]
    tokens, feat = g_ref.shape
    capacity = sent_ref.shape[2]
    first, second = ids_ref[0:1, :], ids_ref[1:2, :]
    row = lax.broadcasted_iota(jnp.int32, (tokens, tokens), 0)
    col = lax.broadcasted_iota(jnp.int32, (tokens, tokens), 1)
    tall_first = jnp.sum(jnp.where(row == col, first, 0), axis=1, keepdims=True)
    tall_second = jnp.sum(jnp.where(row == col, second, 0), axis=1, keepdims=True)

    def slot_of(ids):
        same = (tall_first == ids).astype(jnp.int32) + (tall_second == ids).astype(jnp.int32)
        rank = jnp.sum(jnp.where(row < col, same, 0), axis=0, keepdims=True)
        return ids * capacity + rank

    slot_first, slot_second = slot_of(first), slot_of(second)
    slots_ref[0:1, :] = slot_first
    slots_ref[1:2, :] = slot_second
    want = lax.broadcasted_iota(jnp.int32, (expert_count * capacity, tokens), 0)
    hit_first, hit_second = slot_first == want, slot_second == want
    picker = jnp.where(hit_first | hit_second, 1.0, 0.0).astype(BF16)
    picker_ref[...] = picker
    gates = jnp.where(hit_first, gates_ref[0:1, :], 0.0) + jnp.where(
        hit_second, gates_ref[1:2, :], 0.0
    )
    gate = jnp.sum(gates, axis=1, keepdims=True)
    for k, piece in enumerate(pieces):
        rows = dot(picker, piece[...]).astype(BF16)
        sent_ref[:, k] = rows.reshape(expert_count, capacity, feat)
    scaled = (gate * dot(picker, g_ref[...])).astype(BF16)
    sent_ref[:, len(pieces)] = scaled.reshape(expert_count, capacity, feat)


def run_dispatch(ids, gates, out_grad, pieces, expert_count, capacity):
    tokens, feat = out_grad.shape
    here = pl.BlockSpec(memory_space=pltpu.VMEM)
    return pl.pallas_call(
        functools.partial(dispatch_kernel, expert_count),
        in_specs=[here] * (3 + len(pieces)),
        out_specs=[here] * 3,
        out_shape=[
            jax.ShapeDtypeStruct((expert_count, len(pieces) + 1, capacity, feat), BF16),
            jax.ShapeDtypeStruct((2, tokens), jnp.int32),
            jax.ShapeDtypeStruct((expert_count * capacity, tokens), BF16),
        ],
        compiler_params=pltpu.CompilerParams(vmem_limit_bytes=58 * MIB),
        name="dispatch",
        interpret=INTERPRET,
    )(ids, gates, out_grad, *pieces)


def project_kernel(order_ref, *refs):
    pieces, (wg_ref, wu_ref, gate_ref, up_ref) = refs[:3], refs[3:]
    groups, rows, feat = pieces[0].shape
    gate = up = None
    for k, piece in zip((0, 3, 1), pieces):
        features = piece[...].reshape(groups * rows, feat)
        cols = pl.ds(pl.multiple_of(order_ref[k] * feat, 128), feat)
        g = dot(features, wg_ref[cols, :])
        u = dot(features, wu_ref[cols, :])
        gate = g if gate is None else gate + g
        up = u if up is None else up + u
    gate_ref[...] = gate
    up_ref[...] = up


def run_project(order, c, wg, wu, step_groups):
    groups, rows, feat = c[0].shape
    width, hidden = wg.shape
    step_rows = step_groups * rows
    piece = pl.BlockSpec((step_groups, rows, feat), lambda s, o: (s, 0, 0))
    whole = pl.BlockSpec((width, hidden), lambda s, o: (0, 0))
    result = pl.BlockSpec((step_rows, hidden), lambda s, o: (s, 0))
    return pl.pallas_call(
        project_kernel,
        grid_spec=pltpu.PrefetchScalarGridSpec(
            num_scalar_prefetch=1,
            grid=(groups // step_groups,),
            in_specs=[piece, piece, piece, whole, whole],
            out_specs=[result, result],
        ),
        out_shape=[jax.ShapeDtypeStruct((groups * rows, hidden), F32)] * 2,
        compiler_params=pltpu.CompilerParams(vmem_limit_bytes=58 * MIB),
        name="project",
        interpret=INTERPRET,
    )(order, *c, wg, wu)


def activate_kernel(order_ref, gate_ref, up_ref, early_ref, late_ref, wg_ref, wu_ref, act_ref, slope_ref, linear_ref):
    groups, rows, feat = early_ref.shape
    early = pl.program_id(0) < pl.num_programs(0) // 2
    features = jnp.where(early, early_ref[...], late_ref[...]).reshape(groups * rows, feat)
    gate = gate_ref[...] + dot(features, wg_ref[...])
    up = up_ref[...] + dot(features, wu_ref[...])
    sig = jax.nn.sigmoid(gate)
    linear = gate * sig
    act_ref[...] = (linear * up).astype(BF16)
    slope_ref[...] = up * (sig * (1.0 + gate * (1.0 - sig)))
    linear_ref[...] = linear


def run_activate(order, gate, up, far, wg, wu, step_groups):
    everything, hidden = gate.shape
    rows, feat = far[0].shape[1:]
    step_rows = step_groups * rows
    steps = everything // step_rows
    block = (step_groups, rows, feat)
    straight = pl.BlockSpec((step_rows, hidden), lambda s, o: (s, 0))
    weight = pl.BlockSpec((feat, hidden), lambda s, o: (o[2], 0))
    return pl.pallas_call(
        activate_kernel,
        grid_spec=pltpu.PrefetchScalarGridSpec(
            num_scalar_prefetch=1,
            grid=(steps,),
            in_specs=[
                straight,
                straight,
                pl.BlockSpec(block, lambda s, o: (jnp.minimum(s, steps // 2 - 1), 0, 0)),
                pl.BlockSpec(block, lambda s, o: (jnp.maximum(s - steps // 2, 0), 0, 0)),
                weight,
                weight,
            ],
            out_specs=[straight, straight, straight],
        ),
        out_shape=[
            jax.ShapeDtypeStruct((everything, hidden), BF16),
            jax.ShapeDtypeStruct((everything, hidden), F32),
            jax.ShapeDtypeStruct((everything, hidden), F32),
        ],
        compiler_params=pltpu.CompilerParams(vmem_limit_bytes=58 * MIB),
        name="activate",
        interpret=INTERPRET,
    )(order, gate, up, *far, wg, wu)


def expert_kernel(expert_count, order_ref, slope_ref, linear_ref, x_ref, wg_ref, wu_ref, wd_ref, gg_ref, ug_ref, ring_ref, cross_ref):
    groups, pipes, rows, feat = x_ref.shape
    total = groups * rows
    half = feat // 2
    capacity = rows // expert_count
    act_grad = None
    for k in range(pipes):
        cols = pl.ds(pl.multiple_of(order_ref[k] * feat, 128), feat)
        a = dot(x_ref[:, k].reshape(total, feat), wd_ref[:, cols], NT)
        act_grad = a if act_grad is None else act_grad + a
    gate_grad = (act_grad * slope_ref[...]).astype(BF16)
    up_grad = (act_grad * linear_ref[...]).astype(BF16)
    gg_ref[...] = gate_grad
    ug_ref[...] = up_grad
    for p in range(pipes):
        cols = slice(p * feat, (p + 1) * feat)
        back = (dot(gate_grad, wg_ref[cols, :], NT) + dot(up_grad, wu_ref[cols, :], NT)).astype(BF16)
        for d in range(groups):
            ring_ref[d, p] = back[d * rows : (d + 1) * rows, :half]
            part = back[d * rows : (d + 1) * rows, half:]
            cross_ref[:, p, d * capacity : (d + 1) * capacity, :] = part.reshape(
                expert_count, capacity, half
            )


def run_expert(order, slope, linear, x, wg, wu, wd, expert_count, step_groups):
    groups, pipes, rows, feat = x.shape
    width, hidden = wg.shape
    half = feat // 2
    step_rows = step_groups * rows
    step_slots = step_rows // expert_count
    everything = groups * rows
    whole = lambda shape: pl.BlockSpec(shape, lambda s, o: (0, 0))
    straight = pl.BlockSpec((step_rows, hidden), lambda s, o: (s, 0))
    return pl.pallas_call(
        functools.partial(expert_kernel, expert_count),
        grid_spec=pltpu.PrefetchScalarGridSpec(
            num_scalar_prefetch=1,
            grid=(groups // step_groups,),
            in_specs=[
                straight,
                straight,
                pl.BlockSpec((step_groups, pipes, rows, feat), lambda s, o: (s, 0, 0, 0)),
                whole((width, hidden)),
                whole((width, hidden)),
                whole((hidden, width)),
            ],
            out_specs=[
                straight,
                straight,
                pl.BlockSpec((step_groups, pipes, rows, half), lambda s, o: (s, 0, 0, 0)),
                pl.BlockSpec((expert_count, pipes, step_slots, half), lambda s, o: (0, 0, s, 0)),
            ],
        ),
        out_shape=[jax.ShapeDtypeStruct((everything, hidden), BF16)] * 2
        + [
            jax.ShapeDtypeStruct((groups, pipes, rows, half), BF16),
            jax.ShapeDtypeStruct((expert_count, pipes, everything // expert_count, half), BF16),
        ],
        compiler_params=pltpu.CompilerParams(vmem_limit_bytes=58 * MIB),
        name="expert",
        interpret=INTERPRET,
    )(order, slope, linear, x, wg, wu, wd)


def weight_kernel(order_ref, x_ref, own_ref, before_ref, after_ref, early_ref, late_ref, act_ref, gg_ref, ug_ref, dwg_ref, dwu_ref, dwd_ref):
    groups, _, rows, feat = x_ref.shape
    step = pl.program_id(0)
    cotangent = x_ref[:, 0].reshape(groups * rows, feat)
    dwd_ref[...] = dot(act_ref[...], cotangent, TN).astype(BF16)

    def wide(value):
        features = value.reshape(groups * rows, feat)
        dwg_ref[...] = dot(gg_ref[...], features, TN).astype(BF16).T
        dwu_ref[...] = dot(ug_ref[...], features, TN).astype(BF16).T

    pl.when(step == 0)(lambda: wide(own_ref[...]))
    pl.when(step == 1)(lambda: wide(after_ref[...]))
    pl.when(step == 2)(lambda: wide(jnp.concatenate([early_ref[...], late_ref[...]], axis=0)))
    pl.when(step == 3)(lambda: wide(before_ref[...]))


def run_weights(order, x, c, act, gg, ug):
    groups, pipes, rows, feat = x.shape
    everything, hidden = act.shape
    whole = pl.BlockSpec((everything, hidden), lambda p, o: (0, 0))
    piece = lambda v: pl.BlockSpec(v.shape, lambda p, o: (0, 0, 0))
    return pl.pallas_call(
        weight_kernel,
        grid_spec=pltpu.PrefetchScalarGridSpec(
            num_scalar_prefetch=1,
            grid=(pipes,),
            in_specs=[pl.BlockSpec((groups, 1, rows, feat), lambda p, o: (0, p, 0, 0))]
            + [piece(v) for v in c]
            + [whole] * 3,
            out_specs=[
                pl.BlockSpec((feat, hidden), lambda p, o: (o[p], 0)),
                pl.BlockSpec((feat, hidden), lambda p, o: (o[p], 0)),
                pl.BlockSpec((hidden, feat), lambda p, o: (0, o[p])),
            ],
        ),
        out_shape=[
            jax.ShapeDtypeStruct((pipes * feat, hidden), BF16),
            jax.ShapeDtypeStruct((pipes * feat, hidden), BF16),
            jax.ShapeDtypeStruct((hidden, pipes * feat), BF16),
        ],
        compiler_params=pltpu.CompilerParams(vmem_limit_bytes=58 * MIB),
        name="weights",
        interpret=INTERPRET,
    )(order, x, *c, act, gg, ug)


def combine_kernel(x_ref, slots_ref, out_ref):
    experts, pipes, slots, half = x_ref.shape
    group_count, _, tokens = slots_ref.shape
    capacity = slots // group_count
    want = lax.broadcasted_iota(jnp.int32, (experts * capacity, tokens), 0)
    for d in range(group_count):
        picked = (slots_ref[d, 0:1, :] == want) | (slots_ref[d, 1:2, :] == want)
        chosen = jnp.where(picked, 1.0, 0.0).astype(BF16)
        for p in range(pipes):
            rows = x_ref[:, p, d * capacity : (d + 1) * capacity, :]
            rows = rows.reshape(experts * capacity, half)
            out_ref[p, d * tokens : (d + 1) * tokens, :] = dot(
                chosen, rows, (((0,), (0,)), ((), ()))
            ).astype(BF16)


def total_of(parts):
    total = parts[0].astype(F32)
    for k in range(1, parts.shape[0]):
        total = total + parts[k].astype(F32)
    return total.astype(BF16)


def run_combine(x, slots):
    _, pipes, _, half = x.shape
    group_count, _, tokens = slots.shape
    here = pl.BlockSpec(memory_space=pltpu.VMEM)
    return pl.pallas_call(
        combine_kernel,
        in_specs=[here, here],
        out_specs=here,
        out_shape=jax.ShapeDtypeStruct((pipes, group_count * tokens, half), BF16),
        compiler_params=pltpu.CompilerParams(vmem_limit_bytes=10 * MIB),
        name="combine",
        interpret=INTERPRET,
    )(x, slots)


def shift(x, axis, by):
    count = lax.axis_size(axis)
    return lax.ppermute(x, axis, [(k, (k + by) % count) for k in range(count)])


def place_kernel(at_ref, *refs):
    pieces, out_ref = refs[:-1], refs[-1]
    count = out_ref.shape[0]
    cut = pieces[-2].shape[0]
    for j in range(count - 1):
        out_ref[at_ref[j]] = pieces[j][...]
    out_ref[at_ref[count - 1], :cut] = pieces[-2][...]
    out_ref[at_ref[count - 1], cut:] = pieces[-1][...]


def groups_ring(x):
    rows, width = x.shape
    cut = rows // 2
    up1, down1 = shift(x, "dp", 1), shift(x, "dp", -1)
    up2, down2 = shift(up1, "dp", 1), shift(down1, "dp", -1)
    up3, down3 = shift(up2, "dp", 1), shift(down2, "dp", -1)
    far_up, far_down = shift(up3[:cut], "dp", 1), shift(down3[cut:], "dp", -1)
    count = lax.axis_size("dp")
    at = (lax.axis_index("dp") + jnp.array([0, 1, 2, 3, 5, 6, 7, 4], jnp.int32)) % count
    here = pl.BlockSpec(memory_space=pltpu.VMEM)
    return pl.pallas_call(
        place_kernel,
        in_specs=[pl.BlockSpec(memory_space=pltpu.SMEM)] + [here] * (count + 1),
        out_specs=here,
        out_shape=jax.ShapeDtypeStruct((count, rows, width), BF16),
        compiler_params=pltpu.CompilerParams(vmem_limit_bytes=6 * MIB),
        name="place",
        interpret=INTERPRET,
    )(at, x, down1, down2, down3, up3, up2, up1, far_up, far_down)


def stack_kernel(*refs):
    for k, piece in enumerate(refs[:-1]):
        refs[-1][k] = piece[...]


def run_stack(pieces):
    here = pl.BlockSpec(memory_space=pltpu.VMEM)
    return pl.pallas_call(
        stack_kernel,
        in_specs=[here] * len(pieces),
        out_specs=here,
        out_shape=jax.ShapeDtypeStruct((len(pieces),) + pieces[0].shape, BF16),
        compiler_params=pltpu.CompilerParams(vmem_limit_bytes=6 * MIB),
        name="stack",
        interpret=INTERPRET,
    )(*pieces)


def pipes_ring(x):
    cut = x.shape[0] // 2
    up1, down1 = shift(x, "pipe", 1), shift(x, "pipe", -1)
    far_up, far_down = shift(up1[:cut], "pipe", 1), shift(down1[cut:], "pipe", -1)
    return x, up1, down1, far_up, far_down


def body(tokens, out_grad, gate_values, expert_ids, w_gate, w_up, w_down):
    expert_count = lax.axis_size("expert")
    group_count = lax.axis_size("dp")
    pipe_count = lax.axis_size("pipe")
    token_count, feat = tokens.shape
    capacity = max(token_count // 2, 2 * token_count // expert_count)
    slot_total = expert_count * capacity
    half = feat // 2
    sent, slot_index, picker = run_dispatch(
        expert_ids.T, gate_values.T, out_grad, (tokens,), expert_count, capacity
    )
    received = lax.all_to_all(sent, "expert", split_axis=0, concat_axis=0, tiled=True)
    c = pipes_ring(groups_ring(received[:, 0].reshape(slot_total, feat)))
    own = received[:, 1].reshape(slot_total, feat)
    near = (own, shift(own, "pipe", -1), shift(own, "pipe", 2), shift(own, "pipe", 1))
    near = run_stack(near)
    x = lax.all_gather(near[None], "dp", axis=0, tiled=True)
    order = (lax.axis_index("pipe") + jnp.arange(pipe_count, dtype=jnp.int32)) % pipe_count
    gate, up = run_project(order, c[:3], w_gate[0], w_up[0], group_count // 4)
    act, slope, linear = run_activate(
        order, gate, up, c[3:], w_gate[0], w_up[0], group_count // 4
    )
    gg, ug, ring, cross = run_expert(
        order, slope, linear, x, w_gate[0], w_up[0], w_down[0], expert_count, group_count // 4
    )
    over_groups = lax.psum_scatter(
        ring.reshape(group_count, pipe_count * slot_total, half), "dp", scatter_dimension=0, tiled=True
    )
    crossed = lax.all_to_all(cross, "expert", split_axis=0, concat_axis=0, tiled=True)
    late_index, gg = lax.optimization_barrier((slot_index, gg))
    column_slots = lax.all_gather(late_index[None], "dp", axis=0, tiled=True)
    gate_weight_gradient, up_weight_gradient, grad_down = run_weights(order, x, c, act, gg, ug)
    over_groups, column_slots, grad_down = lax.optimization_barrier(
        (over_groups, column_slots, grad_down)
    )
    summed = lax.psum_scatter(
        over_groups.reshape(pipe_count, slot_total, half), "pipe", scatter_dimension=0, tiled=True
    )
    column = run_combine(crossed, column_slots)
    column = lax.all_to_all(column, "pipe", split_axis=0, concat_axis=0, tiled=True)
    column = total_of(column)
    column = lax.all_to_all(
        column.reshape(group_count, token_count, half),
        "dp",
        split_axis=0,
        concat_axis=0,
        tiled=True,
    )
    right = total_of(column)
    returned = lax.all_to_all(
        summed.reshape(expert_count, capacity, half),
        "expert",
        split_axis=0,
        concat_axis=0,
        tiled=True,
    )
    left = jnp.einsum(
        "st,sq->tq", picker, returned.reshape(slot_total, half), preferred_element_type=F32
    ).astype(BF16)
    grad_tokens = jnp.concatenate([left, right], axis=1)
    return (
        grad_tokens,
        gate_weight_gradient[None],
        up_weight_gradient[None],
        grad_down[None],
    )


def solution(mesh):
    rows = P(("expert", "dp"), "pipe")
    pairs = P(("expert", "dp"), None)
    wide = P("expert", None, ("dp", "pipe"))
    tall = P("expert", ("dp", "pipe"), None)

    return jax.shard_map(
        body,
        mesh=mesh,
        in_specs=(rows, rows, pairs, pairs, wide, wide, tall),
        out_specs=(rows, wide, wide, tall),
        check_vma=False,
    )
```

```python
import functools

import jax
import jax.numpy as jnp
from jax import lax
from jax.experimental import pallas as pl
from jax.experimental.pallas import tpu as pltpu
from jax.sharding import PartitionSpec as P


F32 = jnp.float32
BF16 = jnp.bfloat16
INTERPRET = False
MIB = 1024 * 1024
NN = (((1,), (0,)), ((), ()))
NT = (((1,), (1,)), ((), ()))
TN = (((0,), (0,)), ((), ()))


def dot(a, b, dims=NN):
    return lax.dot_general(a, b, dims, preferred_element_type=F32)


def in_hbm(shape, dtype):
    return jax.ShapeDtypeStruct(shape, dtype) if INTERPRET else pltpu.HBM(shape, dtype)


def dispatch_kernel(expert_count, ids_ref, gates_ref, g_ref, *refs):
    pieces, (sent_ref, slots_ref, picker_ref) = refs[:-3], refs[-3:]
    tokens, feat = g_ref.shape
    capacity = sent_ref.shape[2]
    first, second = ids_ref[0:1, :], ids_ref[1:2, :]
    row = lax.broadcasted_iota(jnp.int32, (tokens, tokens), 0)
    col = lax.broadcasted_iota(jnp.int32, (tokens, tokens), 1)
    tall_first = jnp.sum(jnp.where(row == col, first, 0), axis=1, keepdims=True)
    tall_second = jnp.sum(jnp.where(row == col, second, 0), axis=1, keepdims=True)

    def slot_of(ids):
        same = (tall_first == ids).astype(jnp.int32) + (tall_second == ids).astype(jnp.int32)
        rank = jnp.sum(jnp.where(row < col, same, 0), axis=0, keepdims=True)
        return ids * capacity + rank

    slot_first, slot_second = slot_of(first), slot_of(second)
    slots_ref[0:1, :] = slot_first
    slots_ref[1:2, :] = slot_second
    want = lax.broadcasted_iota(jnp.int32, (expert_count * capacity, tokens), 0)
    hit_first, hit_second = slot_first == want, slot_second == want
    picker = jnp.where(hit_first | hit_second, 1.0, 0.0).astype(BF16)
    picker_ref[...] = picker
    gates = jnp.where(hit_first, gates_ref[0:1, :], 0.0) + jnp.where(
        hit_second, gates_ref[1:2, :], 0.0
    )
    gate = jnp.sum(gates, axis=1, keepdims=True)
    for k, piece in enumerate(pieces):
        rows = dot(picker, piece[...]).astype(BF16)
        sent_ref[:, k] = rows.reshape(expert_count, capacity, feat)
    scaled = (gate * dot(picker, g_ref[...])).astype(BF16)
    sent_ref[:, len(pieces)] = scaled.reshape(expert_count, capacity, feat)


def run_dispatch(ids, gates, out_grad, pieces, expert_count, capacity):
    tokens, feat = out_grad.shape
    here = pl.BlockSpec(memory_space=pltpu.VMEM)
    return pl.pallas_call(
        functools.partial(dispatch_kernel, expert_count),
        in_specs=[here] * (3 + len(pieces)),
        out_specs=[here] * 3,
        out_shape=[
            jax.ShapeDtypeStruct((expert_count, len(pieces) + 1, capacity, feat), BF16),
            jax.ShapeDtypeStruct((2, tokens), jnp.int32),
            jax.ShapeDtypeStruct((expert_count * capacity, tokens), BF16),
        ],
        compiler_params=pltpu.CompilerParams(vmem_limit_bytes=58 * MIB),
        name="dispatch",
        interpret=INTERPRET,
    )(ids, gates, out_grad, *pieces)


def project_kernel(order_ref, *refs):
    pieces, (wg_ref, wu_ref, gate_ref, up_ref) = refs[:3], refs[3:]
    groups, rows, feat = pieces[0].shape
    gate = up = None
    for k, piece in zip((0, 3, 1), pieces):
        features = piece[...].reshape(groups * rows, feat)
        cols = pl.ds(pl.multiple_of(order_ref[k] * feat, 128), feat)
        g = dot(features, wg_ref[cols, :])
        u = dot(features, wu_ref[cols, :])
        gate = g if gate is None else gate + g
        up = u if up is None else up + u
    gate_ref[...] = gate
    up_ref[...] = up


def run_project(order, c, wg, wu, step_groups):
    groups, rows, feat = c[0].shape
    width, hidden = wg.shape
    step_rows = step_groups * rows
    piece = pl.BlockSpec((step_groups, rows, feat), lambda s, o: (s, 0, 0))
    whole = pl.BlockSpec((width, hidden), lambda s, o: (0, 0))
    result = pl.BlockSpec((step_rows, hidden), lambda s, o: (s, 0))
    return pl.pallas_call(
        project_kernel,
        grid_spec=pltpu.PrefetchScalarGridSpec(
            num_scalar_prefetch=1,
            grid=(groups // step_groups,),
            in_specs=[piece, piece, piece, whole, whole],
            out_specs=[result, result],
        ),
        out_shape=[jax.ShapeDtypeStruct((groups * rows, hidden), F32)] * 2,
        compiler_params=pltpu.CompilerParams(vmem_limit_bytes=40 * MIB),
        name="project",
        interpret=INTERPRET,
    )(order, *c, wg, wu)


def activate_kernel(order_ref, gate_ref, up_ref, early_ref, late_ref, wg_ref, wu_ref, act_ref, slope_ref, linear_ref):
    groups, rows, feat = early_ref.shape
    early = pl.program_id(0) < pl.num_programs(0) // 2
    features = jnp.where(early, early_ref[...], late_ref[...]).reshape(groups * rows, feat)
    gate = gate_ref[...] + dot(features, wg_ref[...])
    up = up_ref[...] + dot(features, wu_ref[...])
    sig = jax.nn.sigmoid(gate)
    linear = gate * sig
    act_ref[...] = (linear * up).astype(BF16)
    slope_ref[...] = up * (sig * (1.0 + gate * (1.0 - sig)))
    linear_ref[...] = linear


def run_activate(order, gate, up, far, wg, wu, step_groups):
    everything, hidden = gate.shape
    rows, feat = far[0].shape[1:]
    step_rows = step_groups * rows
    steps = everything // step_rows
    block = (step_groups, rows, feat)
    straight = pl.BlockSpec((step_rows, hidden), lambda s, o: (s, 0))
    weight = pl.BlockSpec((feat, hidden), lambda s, o: (o[2], 0))
    return pl.pallas_call(
        activate_kernel,
        grid_spec=pltpu.PrefetchScalarGridSpec(
            num_scalar_prefetch=1,
            grid=(steps,),
            in_specs=[
                straight,
                straight,
                pl.BlockSpec(block, lambda s, o: (jnp.minimum(s, steps // 2 - 1), 0, 0)),
                pl.BlockSpec(block, lambda s, o: (jnp.maximum(s - steps // 2, 0), 0, 0)),
                weight,
                weight,
            ],
            out_specs=[straight, straight, straight],
        ),
        out_shape=[
            in_hbm((everything, hidden), BF16),
            in_hbm((everything, hidden), F32),
            in_hbm((everything, hidden), F32),
        ],
        compiler_params=pltpu.CompilerParams(vmem_limit_bytes=24 * MIB),
        name="activate",
        interpret=INTERPRET,
    )(order, gate, up, *far, wg, wu)


def expert_kernel(expert_count, order_ref, slope_ref, linear_ref, x_ref, wg_ref, wu_ref, wd_ref, gg_ref, ug_ref, ring_ref, cross_ref):
    groups, pipes, rows, feat = x_ref.shape
    total = groups * rows
    half = feat // 2
    capacity = rows // expert_count
    act_grad = None
    for k in range(pipes):
        cols = pl.ds(pl.multiple_of(order_ref[k] * feat, 128), feat)
        a = dot(x_ref[:, k].reshape(total, feat), wd_ref[:, cols], NT)
        act_grad = a if act_grad is None else act_grad + a
    gate_grad = (act_grad * slope_ref[...]).astype(BF16)
    up_grad = (act_grad * linear_ref[...]).astype(BF16)
    gg_ref[...] = gate_grad
    ug_ref[...] = up_grad
    for p in range(pipes):
        cols = slice(p * feat, (p + 1) * feat)
        back = (dot(gate_grad, wg_ref[cols, :], NT) + dot(up_grad, wu_ref[cols, :], NT)).astype(BF16)
        for d in range(groups):
            ring_ref[d, p] = back[d * rows : (d + 1) * rows, :half]
            part = back[d * rows : (d + 1) * rows, half:]
            cross_ref[:, p, d * capacity : (d + 1) * capacity, :] = part.reshape(
                expert_count, capacity, half
            )


def run_expert(order, slope, linear, x, wg, wu, wd, expert_count, step_groups):
    groups, pipes, rows, feat = x.shape
    width, hidden = wg.shape
    half = feat // 2
    step_rows = step_groups * rows
    step_slots = step_rows // expert_count
    everything = groups * rows
    whole = lambda shape: pl.BlockSpec(shape, lambda s, o: (0, 0))
    straight = pl.BlockSpec((step_rows, hidden), lambda s, o: (s, 0))
    return pl.pallas_call(
        functools.partial(expert_kernel, expert_count),
        grid_spec=pltpu.PrefetchScalarGridSpec(
            num_scalar_prefetch=1,
            grid=(groups // step_groups,),
            in_specs=[
                straight,
                straight,
                pl.BlockSpec((step_groups, pipes, rows, feat), lambda s, o: (s, 0, 0, 0)),
                whole((width, hidden)),
                whole((width, hidden)),
                whole((hidden, width)),
            ],
            out_specs=[
                straight,
                straight,
                pl.BlockSpec((step_groups, pipes, rows, half), lambda s, o: (s, 0, 0, 0)),
                pl.BlockSpec((expert_count, pipes, step_slots, half), lambda s, o: (0, 0, s, 0)),
            ],
        ),
        out_shape=[jax.ShapeDtypeStruct((everything, hidden), BF16)] * 2
        + [
            jax.ShapeDtypeStruct((groups, pipes, rows, half), BF16),
            jax.ShapeDtypeStruct((expert_count, pipes, everything // expert_count, half), BF16),
        ],
        compiler_params=pltpu.CompilerParams(vmem_limit_bytes=58 * MIB),
        name="expert",
        interpret=INTERPRET,
    )(order, slope, linear, x, wg, wu, wd)


def weight_kernel(order_ref, x_ref, own_ref, before_ref, after_ref, early_ref, late_ref, act_ref, gg_ref, ug_ref, dwg_ref, dwu_ref, dwd_ref):
    groups, _, rows, feat = x_ref.shape
    step = pl.program_id(0)
    cotangent = x_ref[:, 0].reshape(groups * rows, feat)
    dwd_ref[...] = dot(act_ref[...], cotangent, TN).astype(BF16)

    def wide(value):
        features = value.reshape(groups * rows, feat)
        dwg_ref[...] = dot(gg_ref[...], features, TN).astype(BF16).T
        dwu_ref[...] = dot(ug_ref[...], features, TN).astype(BF16).T

    pl.when(step == 0)(lambda: wide(own_ref[...]))
    pl.when(step == 1)(lambda: wide(after_ref[...]))
    pl.when(step == 2)(lambda: wide(jnp.concatenate([early_ref[...], late_ref[...]], axis=0)))
    pl.when(step == 3)(lambda: wide(before_ref[...]))


def run_weights(order, x, c, act, gg, ug):
    groups, pipes, rows, feat = x.shape
    everything, hidden = act.shape
    whole = pl.BlockSpec((everything, hidden), lambda p, o: (0, 0))
    piece = lambda v: pl.BlockSpec(v.shape, lambda p, o: (0, 0, 0))
    return pl.pallas_call(
        weight_kernel,
        grid_spec=pltpu.PrefetchScalarGridSpec(
            num_scalar_prefetch=1,
            grid=(pipes,),
            in_specs=[pl.BlockSpec((groups, 1, rows, feat), lambda p, o: (0, p, 0, 0))]
            + [piece(v) for v in c]
            + [whole] * 3,
            out_specs=[
                pl.BlockSpec((feat, hidden), lambda p, o: (o[p], 0)),
                pl.BlockSpec((feat, hidden), lambda p, o: (o[p], 0)),
                pl.BlockSpec((hidden, feat), lambda p, o: (0, o[p])),
            ],
        ),
        out_shape=[
            jax.ShapeDtypeStruct((pipes * feat, hidden), BF16),
            jax.ShapeDtypeStruct((pipes * feat, hidden), BF16),
            jax.ShapeDtypeStruct((hidden, pipes * feat), BF16),
        ],
        compiler_params=pltpu.CompilerParams(vmem_limit_bytes=58 * MIB),
        name="weights",
        interpret=INTERPRET,
    )(order, x, *c, act, gg, ug)


def combine_kernel(x_ref, slots_ref, out_ref):
    experts, pipes, slots, half = x_ref.shape
    group_count, _, tokens = slots_ref.shape
    capacity = slots // group_count
    want = lax.broadcasted_iota(jnp.int32, (experts * capacity, tokens), 0)
    for d in range(group_count):
        picked = (slots_ref[d, 0:1, :] == want) | (slots_ref[d, 1:2, :] == want)
        chosen = jnp.where(picked, 1.0, 0.0).astype(BF16)
        for p in range(pipes):
            rows = x_ref[:, p, d * capacity : (d + 1) * capacity, :]
            rows = rows.reshape(experts * capacity, half)
            out_ref[p, d * tokens : (d + 1) * tokens, :] = dot(
                chosen, rows, (((0,), (0,)), ((), ()))
            ).astype(BF16)


def total_of(parts):
    total = parts[0].astype(F32)
    for k in range(1, parts.shape[0]):
        total = total + parts[k].astype(F32)
    return total.astype(BF16)


def run_combine(x, slots):
    _, pipes, _, half = x.shape
    group_count, _, tokens = slots.shape
    here = pl.BlockSpec(memory_space=pltpu.VMEM)
    return pl.pallas_call(
        combine_kernel,
        in_specs=[here, here],
        out_specs=here,
        out_shape=jax.ShapeDtypeStruct((pipes, group_count * tokens, half), BF16),
        compiler_params=pltpu.CompilerParams(vmem_limit_bytes=10 * MIB),
        name="combine",
        interpret=INTERPRET,
    )(x, slots)


def shift(x, axis, by):
    count = lax.axis_size(axis)
    return lax.ppermute(x, axis, [(k, (k + by) % count) for k in range(count)])


def place_kernel(at_ref, *refs):
    pieces, out_ref = refs[:-1], refs[-1]
    count = out_ref.shape[0]
    cut = pieces[-2].shape[0]
    for j in range(count - 1):
        out_ref[at_ref[j]] = pieces[j][...]
    out_ref[at_ref[count - 1], :cut] = pieces[-2][...]
    out_ref[at_ref[count - 1], cut:] = pieces[-1][...]


def groups_ring(x):
    rows, width = x.shape
    cut = rows // 2
    up1, down1 = shift(x, "dp", 1), shift(x, "dp", -1)
    up2, down2 = shift(up1, "dp", 1), shift(down1, "dp", -1)
    up3, down3 = shift(up2, "dp", 1), shift(down2, "dp", -1)
    far_up, far_down = shift(up3[:cut], "dp", 1), shift(down3[cut:], "dp", -1)
    count = lax.axis_size("dp")
    at = (lax.axis_index("dp") + jnp.array([0, 1, 2, 3, 5, 6, 7, 4], jnp.int32)) % count
    here = pl.BlockSpec(memory_space=pltpu.VMEM)
    return pl.pallas_call(
        place_kernel,
        in_specs=[pl.BlockSpec(memory_space=pltpu.SMEM)] + [here] * (count + 1),
        out_specs=here,
        out_shape=jax.ShapeDtypeStruct((count, rows, width), BF16),
        compiler_params=pltpu.CompilerParams(vmem_limit_bytes=6 * MIB),
        name="place",
        interpret=INTERPRET,
    )(at, x, down1, down2, down3, up3, up2, up1, far_up, far_down)


def stack_kernel(*refs):
    for k, piece in enumerate(refs[:-1]):
        refs[-1][k] = piece[...]


def run_stack(pieces):
    here = pl.BlockSpec(memory_space=pltpu.VMEM)
    return pl.pallas_call(
        stack_kernel,
        in_specs=[here] * len(pieces),
        out_specs=here,
        out_shape=jax.ShapeDtypeStruct((len(pieces),) + pieces[0].shape, BF16),
        compiler_params=pltpu.CompilerParams(vmem_limit_bytes=6 * MIB),
        name="stack",
        interpret=INTERPRET,
    )(*pieces)


def pipes_ring(x):
    cut = x.shape[0] // 2
    up1, down1 = shift(x, "pipe", 1), shift(x, "pipe", -1)
    far_up, far_down = shift(up1[:cut], "pipe", 1), shift(down1[cut:], "pipe", -1)
    return x, up1, down1, far_up, far_down


def body(tokens, out_grad, gate_values, expert_ids, w_gate, w_up, w_down):
    expert_count = lax.axis_size("expert")
    group_count = lax.axis_size("dp")
    pipe_count = lax.axis_size("pipe")
    token_count, feat = tokens.shape
    capacity = max(token_count // 2, 2 * token_count // expert_count)
    slot_total = expert_count * capacity
    half = feat // 2
    sent, slot_index, picker = run_dispatch(
        expert_ids.T, gate_values.T, out_grad, (tokens,), expert_count, capacity
    )
    received = lax.all_to_all(sent, "expert", split_axis=0, concat_axis=0, tiled=True)
    c = pipes_ring(groups_ring(received[:, 0].reshape(slot_total, feat)))
    own = received[:, 1].reshape(slot_total, feat)
    near = (own, shift(own, "pipe", -1), shift(own, "pipe", 2), shift(own, "pipe", 1))
    near = run_stack(near)
    x = lax.all_gather(near[None], "dp", axis=0, tiled=True)
    order = (lax.axis_index("pipe") + jnp.arange(pipe_count, dtype=jnp.int32)) % pipe_count
    gate, up = run_project(order, c[:3], w_gate[0], w_up[0], group_count // 4)
    act, slope, linear = run_activate(
        order, gate, up, c[3:], w_gate[0], w_up[0], group_count // 2
    )
    gg, ug, ring, cross = run_expert(
        order, slope, linear, x, w_gate[0], w_up[0], w_down[0], expert_count, group_count // 4
    )
    over_groups = lax.psum_scatter(
        ring.reshape(group_count, pipe_count * slot_total, half), "dp", scatter_dimension=0, tiled=True
    )
    crossed = lax.all_to_all(cross, "expert", split_axis=0, concat_axis=0, tiled=True)
    late_index, gg = lax.optimization_barrier((slot_index, gg))
    column_slots = lax.all_gather(late_index[None], "dp", axis=0, tiled=True)
    gate_weight_gradient, up_weight_gradient, grad_down = run_weights(order, x, c, act, gg, ug)
    over_groups, column_slots, grad_down = lax.optimization_barrier(
        (over_groups, column_slots, grad_down)
    )
    summed = lax.psum_scatter(
        over_groups.reshape(pipe_count, slot_total, half), "pipe", scatter_dimension=0, tiled=True
    )
    column = run_combine(crossed, column_slots)
    column = lax.all_to_all(column, "pipe", split_axis=0, concat_axis=0, tiled=True)
    column = total_of(column)
    column = lax.all_to_all(
        column.reshape(group_count, token_count, half),
        "dp",
        split_axis=0,
        concat_axis=0,
        tiled=True,
    )
    right = total_of(column)
    returned = lax.all_to_all(
        summed.reshape(expert_count, capacity, half),
        "expert",
        split_axis=0,
        concat_axis=0,
        tiled=True,
    )
    left = jnp.einsum(
        "st,sq->tq", picker, returned.reshape(slot_total, half), preferred_element_type=F32
    ).astype(BF16)
    grad_tokens = jnp.concatenate([left, right], axis=1)
    return (
        grad_tokens,
        gate_weight_gradient[None],
        up_weight_gradient[None],
        grad_down[None],
    )


def solution(mesh):
    rows = P(("expert", "dp"), "pipe")
    pairs = P(("expert", "dp"), None)
    wide = P("expert", None, ("dp", "pipe"))
    tall = P("expert", ("dp", "pipe"), None)

    return jax.shard_map(
        body,
        mesh=mesh,
        in_specs=(rows, rows, pairs, pairs, wide, wide, tall),
        out_specs=(rows, wide, wide, tall),
        check_vma=False,
    )
```
